128 devices in a mesh: strip: 8 (over x, y_lo), along: 16 (over z, y_hi, core).
Axes of the slice: x: 4, y: 4 (y_hi: 2, y_lo: 2; y = y_hi * 2 + y_lo), z: 4, core: 2. Of those that a mesh axis runs over, the one named last changes fastest.
Arguments:
- images: float32 [512, 8192], P('strip', 'along'), may hold values from 0 to 255
- offsets: int32 [8, 16, 2], P('strip', 'along'), may hold values from 0 to 31
Outputs:
- matches: float32 [8, 512, 8192], P(None, 'strip', 'along')
The draws below stay inside these ranges and needn't reach their ends.
All inputs are finite; a program needn't handle non-finite values.
Results may differ from the reference program's by a relative error of at most 0.000063.
Values sent between devices are 32-bit elements; how exact they have to be, the bound alone decides.
A program may use at most 64 MiB of HBM per device.

```python
import jax
import jax.numpy as jnp
from jax import lax

ROWS = 64
COLS = 512
DISP = 16
NROWS = 512
NCOLS = 8192
N_STRIP = 8
N_ALONG = 16


def touch_ends(drawn, rng, low, largest):
    shape = drawn.shape
    spot = [jax.random.randint(jax.random.fold_in(rng, axis), (), 0, shape[axis]) for axis in range(len(shape))]
    drawn = drawn.at[tuple(spot)].set(low)
    longest = shape.index(max(shape))
    spot[longest] = (spot[longest] + 1) % shape[longest]
    return drawn.at[tuple(spot)].set(largest)


def shard_levels(stream_key, shape, split, smallest, largest):
    def one(dim, shards_of):
        heights = jax.random.uniform(jax.random.fold_in(jax.random.fold_in(stream_key, 6), dim), (shards_of,), jnp.float32, smallest / len(split), largest / len(split))
        return jnp.repeat(jnp.exp(heights), shape[dim] // shards_of).reshape((-1,) + (1,) * (len(shape) - dim - 1))

    loudness = one(*split[0])
    for cut in split[1:]:
        loudness = loudness * one(*cut)
    return loudness


def setup_inputs(seed: int = 0) -> dict:
    key_list = jax.random.split(jax.random.key(seed), 3)
    return {
        "images": jnp.clip(255.0 * jax.random.uniform(key_list[0], (NROWS, NCOLS), jnp.float32) ** shard_levels(key_list[0], (NROWS, NCOLS), ((0, 8), (1, 16)), -0.2, 0.2), 0.0, 255.0),
        "offsets": touch_ends(jax.random.randint(key_list[1], (N_STRIP, N_ALONG, 2), 0, min(ROWS, COLS) // 2), jax.random.fold_in(key_list[1], 1), 0, (min(ROWS, COLS) // 2) - 1).astype(jnp.int32),
    }


box_radius = 4


def box_sum(field):
    height, width = field.shape
    padded = jnp.pad(field, ((box_radius, box_radius), (0, 0)))
    rows_total = padded[0:height]
    for shift_k in range(1, 2 * box_radius + 1):
        rows_total = rows_total + padded[shift_k:shift_k + height]
    padded = jnp.pad(rows_total, ((0, 0), (box_radius, box_radius)))
    total = padded[:, 0:width]
    for shift_k in range(1, 2 * box_radius + 1):
        total = total + padded[:, shift_k:shift_k + width]
    return total


def pair_maps(guide, partner, roll_axis, base):
    counts = box_sum(jnp.ones_like(guide))
    mean_g = box_sum(guide) / counts
    var_g = box_sum(guide * guide) / counts - mean_g * mean_g
    filtered = []
    for level in range(DISP):
        shifted = jnp.roll(partner, -(base + level), axis=roll_axis)
        cost = jnp.abs(guide - shifted)
        mean_p = box_sum(cost) / counts
        cov = box_sum(guide * cost) / counts - mean_g * mean_p
        coef_a = cov / (var_g + 50.0)
        coef_b = mean_p - coef_a * mean_g
        filtered.append(box_sum(coef_a) / counts * guide + box_sum(coef_b) / counts)
    scores = -jnp.stack(filtered) * 4.0
    top = jnp.max(scores, axis=0)
    weights = jnp.exp(scores - top)
    prob = weights / jnp.sum(weights, axis=0)
    levels = jnp.arange(DISP).astype(jnp.float32)[:, None, None]
    disparity = jnp.sum(levels * prob, axis=0)
    confidence = jnp.sum(prob * prob, axis=0)
    return jnp.stack([disparity, confidence])


def reference(images, offsets):
    blocks = images.reshape(N_STRIP, ROWS, N_ALONG, COLS).transpose(0, 2, 1, 3)
    zeros_col = jnp.zeros((N_STRIP, 1, ROWS, COLS), jnp.float32)
    zeros_row = jnp.zeros((1, N_ALONG, ROWS, COLS), jnp.float32)
    forward = jnp.concatenate([blocks[:, 1:], zeros_col], axis=1)
    side = jnp.concatenate([blocks[1:], zeros_row], axis=0)
    count = N_STRIP * N_ALONG

    def one_block(items):
        guide, fwd_part, side_part, shift_pair = items
        return jnp.concatenate([pair_maps(guide, fwd_part, 1, shift_pair[0]), pair_maps(guide, side_part, 0, shift_pair[1])])

    maps = lax.map(one_block, (blocks.reshape(count, ROWS, COLS), forward.reshape(count, ROWS, COLS), side.reshape(count, ROWS, COLS), offsets.reshape(count, 2)))
    maps = maps.reshape(N_STRIP, N_ALONG, 4, ROWS, COLS)
    fwd_own = maps[:, :, 0:2]
    side_own = maps[:, :, 2:4]
    fwd_back = jnp.concatenate([jnp.zeros_like(fwd_own[:, 0:1]), fwd_own[:, :-1]], axis=1)
    side_back = jnp.concatenate([jnp.zeros_like(side_own[0:1]), side_own[:-1]], axis=0)
    full = jnp.concatenate([fwd_own, fwd_back, side_own, side_back], axis=2)
    return full.transpose(2, 0, 3, 1, 4).reshape(8, N_STRIP * ROWS, N_ALONG * COLS)
```

```python
import functools
import jax
import jax.numpy as jnp
from jax import lax
from jax.experimental import pallas as pl
from jax.experimental.pallas import tpu as pltpu
from jax.sharding import PartitionSpec as P

F32 = jnp.float32
BF16 = jnp.bfloat16
ROWS, COLS, GROUPS, SUB, LANES = 64, 512, 8, 8, 128
HALF = LANES // 2
RADIUS = 4
UNROLL = 16
SCALE = -4.0 * 1.4426950408889634


def lane_ids(shape):
    return lax.broadcasted_iota(jnp.int32, shape, len(shape) - 1)


def split3(x):
    hi = x.astype(BF16)
    rest = x - hi.astype(F32)
    mid = rest.astype(BF16)
    low = (rest - mid.astype(F32)).astype(BF16)
    return jnp.concatenate([hi, mid, low], axis=0)


def permuted(x, perm, transposed):
    n = x.shape[0]
    dims = (((1,), (1 if transposed else 0,)), ((), ()))
    out = lax.dot_general(split3(x), perm, dims, preferred_element_type=F32)
    return out[:n] + out[n : 2 * n] + out[2 * n :]


def fill_perm(perm_ref):
    for k in range(4):
        shape = (128, COLS)
        n = lax.broadcasted_iota(jnp.int32, shape, 1)
        c = lax.broadcasted_iota(jnp.int32, shape, 0) + 128 * k
        hit = c == 8 * (n & 63) + (n >> 6)
        perm_ref[pl.ds(128 * k, 128), :] = jnp.where(hit, 1.0, 0.0).astype(BF16)


def spread(x, perm):
    y = permuted(x, perm, False)
    low = lane_ids((x.shape[0], LANES)) < HALF
    out = []
    for k in range(4):
        v = y[:, LANES * k : LANES * (k + 1)]
        w = pltpu.roll(v, HALF, 1)
        out += [jnp.where(low, v, w), jnp.where(low, w, v)]
    return out


def row_box(x):
    shape = x[0].shape
    pos = lane_ids(shape) & (HALF - 1)
    first, last = pos == 0, pos == HALF - 1
    pre = [x[0]]
    for k in range(1, 8):
        pre.append(pre[-1] + x[k])
    suf = [None] * 8
    suf[7] = x[7]
    for k in range(6, 0, -1):
        suf[k] = suf[k + 1] + x[k]
    suf[0] = pre[7]
    out = []
    for j in range(4):
        out.append(jnp.where(first, 0.0, pltpu.roll(suf[j + 4], 1, 1)) + pre[j + 4])
    for j in range(4, 8):
        out.append(jnp.where(last, 0.0, pltpu.roll(pre[j - 4], LANES - 1, 1)) + suf[j - 4])
    return out


def guide_fields(g, perm, pad_ref, g_ref, a1_ref, a2_ref, i4_ref, mg_ref, inv_ref):
    gd = spread(g, perm)
    zero = jnp.zeros((SUB, LANES), F32)
    for j in range(8):
        g_ref[j] = gd[j]
        for n, field in enumerate((gd[j], gd[j] * gd[j])):
            at = 2 * j + n
            pad_ref[at, pl.ds(0, SUB), :] = zero
            pad_ref[at, pl.ds(SUB, ROWS), :] = field
            pad_ref[at, pl.ds(SUB + ROWS, SUB), :] = zero

    def tile(i, carry):
        base = pl.multiple_of(i * SUB, SUB)
        sums = []
        for at in range(16):
            total = pad_ref[at, pl.ds(base + SUB - RADIUS, SUB), :]
            for k in range(1, 2 * RADIUS + 1):
                total = total + pad_ref[at, pl.ds(base + SUB - RADIUS + k, SUB), :]
            sums.append(total)
        bg, bgg = row_box(sums[0::2]), row_box(sums[1::2])
        shape = (SUB, LANES)
        r = lax.broadcasted_iota(jnp.int32, shape, 0) + base
        nr = jnp.minimum(r + RADIUS, ROWS - 1) - jnp.maximum(r - RADIUS, 0) + 1
        l8 = 8 * (lane_ids(shape) & (HALF - 1))
        for j in range(8):
            c = l8 + j
            nc = jnp.minimum(c + RADIUS, COLS - 1) - jnp.maximum(c - RADIUS, 0) + 1
            inv = 1.0 / (nr * nc).astype(F32)
            mean = bg[j] * inv
            var = bgg[j] * inv - mean * mean
            a1 = (SCALE * inv) / (var + 50.0)
            here = pl.ds(base, SUB)
            a1_ref[j, here, :] = a1
            a2_ref[j, here, :] = a1 * mean
            i4_ref[j, here, :] = SCALE * inv
            mg_ref[j, here, :] = mean
            inv_ref[j, here, :] = inv
        return carry

    lax.fori_loop(0, ROWS // SUB, tile, 0)


def forward_table(f, shift, perm, z_ref):
    base = spread(pltpu.roll(f, COLS - shift, 1), perm)
    low = lane_ids((ROWS, LANES)) < HALF
    for e in range(8):
        one = pltpu.roll(base[e], LANES - 1, 1)
        two = pltpu.roll(one, LANES - 1, 1)
        z_ref[pl.ds(e, ROWS, stride=16), :] = jnp.where(low, base[e], one)
        z_ref[pl.ds(e + 8, ROWS, stride=16), :] = jnp.where(low, one, two)


def side_table(s, shift, perm, y_ref, pad_ref):
    base = spread(pltpu.roll(s, ROWS - shift, 0), perm)
    low = lane_ids((SUB, LANES)) < HALF
    for j in range(8):
        tiles = [base[j][SUB * k : SUB * (k + 1)] for k in range(8)]
        for k in range(9):
            y_ref[j, pl.ds(SUB * k, SUB), :] = jnp.where(low, tiles[k % 8], tiles[(k + 1) % 8])


def bcast(ref, j, r):
    return jnp.broadcast_to(ref[j, pl.ds(r, 1), :], (SUB, LANES))


def cost_pass(load, g_ref, hx_ref, hy_ref):
    def row(r, carry):
        xs, ys = [], []
        for j in range(8):
            g = bcast(g_ref, j, r)
            x = jnp.abs(g - load(r, j))
            xs.append(x)
            ys.append(g * x)
        for ref, vals in ((hx_ref, xs), (hy_ref, ys)):
            for j, v in enumerate(row_box(vals)):
                ref[j, r] = v
        return carry

    lax.fori_loop(0, ROWS, row, 0, unroll=UNROLL)


def coef_pass(hx_ref, hy_ref, wa_ref, wb_ref, a1_ref, a2_ref, i4_ref, mg_ref):
    def column(j, carry):
        def window(ref):
            total = ref[j, 0]
            for r in range(1, RADIUS):
                total = total + ref[j, r]
            return total

        p, q = window(hx_ref), window(hy_ref)
        olda, oldb = [], []
        wa = wb = None
        for r in range(ROWS + RADIUS):
            if r < ROWS:
                if r + RADIUS < ROWS:
                    if r > RADIUS:
                        p = p + (hx_ref[j, r + RADIUS] - hx_ref[j, r - RADIUS - 1])
                        q = q + (hy_ref[j, r + RADIUS] - hy_ref[j, r - RADIUS - 1])
                    else:
                        p = p + hx_ref[j, r + RADIUS]
                        q = q + hy_ref[j, r + RADIUS]
                else:
                    p = p - hx_ref[j, r - RADIUS - 1]
                    q = q - hy_ref[j, r - RADIUS - 1]
                ca = q * bcast(a1_ref, j, r) - p * bcast(a2_ref, j, r)
                cb = p * bcast(i4_ref, j, r) - ca * bcast(mg_ref, j, r)
                olda.append(ca)
                oldb.append(cb)
                if r == 0:
                    wa, wb = ca, cb
                elif r > 2 * RADIUS:
                    wa = wa + (ca - olda[r - 2 * RADIUS - 1])
                    wb = wb + (cb - oldb[r - 2 * RADIUS - 1])
                else:
                    wa, wb = wa + ca, wb + cb
            else:
                wa = wa - olda[r - 2 * RADIUS - 1]
                wb = wb - oldb[r - 2 * RADIUS - 1]
            if r >= RADIUS:
                wa_ref[j, r - RADIUS] = wa
                wb_ref[j, r - RADIUS] = wb
        return carry

    lax.fori_loop(0, 8, column, 0)


def score_pass(wa_ref, wb_ref, g_ref, inv_ref, sc_ref):
    def row(r, carry):
        ha = row_box([wa_ref[j, r] for j in range(8)])
        hb = row_box([wb_ref[j, r] for j in range(8)])
        for j in range(8):
            sc_ref[r, pl.ds(SUB * j, SUB), :] = (ha[j] * bcast(g_ref, j, r) + hb[j]) * bcast(inv_ref, j, r)
        return carry

    lax.fori_loop(0, ROWS, row, 0, unroll=UNROLL)


def softmax_pass(sc_ref, d_ref, c_ref):
    def row(r, carry):
        high = lane_ids((SUB, LANES)) >= HALF
        t = [sc_ref[r, pl.ds(s, SUB, stride=SUB), :] for s in range(8)]
        top = t[0]
        for s in range(1, 8):
            top = jnp.maximum(top, t[s])
        top = jnp.maximum(top, pltpu.roll(top, HALF, 1))
        total = lift = square = None
        for s in range(7, -1, -1):
            w = jnp.exp2(t[s] - top)
            total = w if total is None else total + w
            square = w * w if square is None else square + w * w
            if s:
                lift = total if lift is None else lift + total
        lift = lift + jnp.where(high, 8.0 * total, 0.0)
        total = total + pltpu.roll(total, HALF, 1)
        lift = lift + pltpu.roll(lift, HALF, 1)
        square = square + pltpu.roll(square, HALF, 1)
        unit = 1.0 / total
        d_ref[pl.ds(pl.multiple_of(r * SUB, SUB), SUB), :] = lift * unit
        c_ref[pl.ds(pl.multiple_of(r * SUB, SUB), SUB), :] = square * unit * unit
        return carry

    lax.fori_loop(0, ROWS, row, 0, unroll=UNROLL)


def gathered(ref, perm):
    low = lane_ids((ROWS, LANES)) < HALF
    parts = []
    for k in range(4):
        even = ref[pl.ds(2 * k, ROWS, stride=SUB), :]
        odd = ref[pl.ds(2 * k + 1, ROWS, stride=SUB), :]
        parts.append(jnp.where(low, even, odd))
    return permuted(jnp.concatenate(parts, axis=1), perm, True)


SCRATCH = dict(
    perm=((COLS, COLS), BF16), pad=((16, ROWS + 16, LANES), F32),
    g=((8, ROWS, LANES), F32), a1=((8, ROWS, LANES), F32), a2=((8, ROWS, LANES), F32),
    i4=((8, ROWS, LANES), F32), mg=((8, ROWS, LANES), F32), inv=((8, ROWS, LANES), F32),
    z=((16 * ROWS, LANES), F32), y=((8, ROWS + SUB, LANES), F32),
    hx=((8, ROWS, SUB, LANES), F32), hy=((8, ROWS, SUB, LANES), F32),
    wa=((8, ROWS, SUB, LANES), F32), wb=((8, ROWS, SUB, LANES), F32),
    sc=((ROWS, SUB * SUB, LANES), F32), d=((ROWS * SUB, LANES), F32), c=((ROWS * SUB, LANES), F32),
)


def levels(load, b):
    cost_pass(load, b["g"], b["hx"], b["hy"])
    coef_pass(b["hx"], b["hy"], b["wa"], b["wb"], b["a1"], b["a2"], b["i4"], b["mg"])
    score_pass(b["wa"], b["wb"], b["g"], b["inv"], b["sc"])
    softmax_pass(b["sc"], b["d"], b["c"])


def load_forward(b):
    return lambda r, j: b["z"][pl.ds(r * 16 + j, SUB), :]


def load_side(b):
    return lambda r, j: b["y"][j, pl.ds(r, SUB), :]
def kernel(t_ref, g_ref, f_ref, s_ref, o_ref, *bufs):
    b = dict(zip(SCRATCH, bufs))
    perm = b["perm"]
    fill_perm(perm)
    guide_fields(g_ref[...], perm[...], b["pad"], b["g"], b["a1"], b["a2"], b["i4"], b["mg"], b["inv"])
    forward_table(f_ref[...], t_ref[0], perm[...], b["z"])
    levels(load_forward(b), b)
    o_ref[0] = gathered(b["d"], perm[...])
    o_ref[1] = gathered(b["c"], perm[...])
    side_table(s_ref[...], t_ref[1], perm[...], b["y"], b["pad"])
    levels(load_side(b), b)
    o_ref[2] = gathered(b["d"], perm[...])
    o_ref[3] = gathered(b["c"], perm[...])

def maps(t, g, f, s):
    V = pl.BlockSpec(memory_space=pltpu.VMEM)
    return pl.pallas_call(kernel, out_shape=jax.ShapeDtypeStruct((4, ROWS, COLS), F32),
        in_specs=[pl.BlockSpec(memory_space=pltpu.SMEM), V, V, V], out_specs=V,
        scratch_shapes=[pltpu.VMEM(*v) for v in SCRATCH.values()],
        compiler_params=pltpu.CompilerParams(vmem_limit_bytes=60 << 20))(t, g, f, s)


def from_behind(value, axis, steps):
    count = lax.axis_size(axis)
    leading, last = (max(0, -steps), min(count, count - steps))
    return lax.ppermute(value, axis, [(source, source + steps) for source in range(leading, last)])


def per_device(images, offsets):
    forward = from_behind(images, "along", -1)
    side = from_behind(images, "strip", -1)
    own = maps(offsets.reshape(2), images, forward, side)
    fwd_back = from_behind(own[0:2], "along", 1)
    side_back = from_behind(own[2:4], "strip", 1)
    return jnp.concatenate([own[0:2], fwd_back, own[2:4], side_back], axis=0)


def solution(mesh):
    placed = (P("strip", "along"), P("strip", "along", None))
    return jax.shard_map(
        per_device, mesh=mesh, in_specs=placed, out_specs=P(None, "strip", "along"), check_vma=False
    )
```

```python
import functools
import jax
import jax.numpy as jnp
from jax import lax
from jax.experimental import pallas as pl
from jax.experimental.pallas import tpu as pltpu
from jax.sharding import PartitionSpec as P

F32 = jnp.float32
BF16 = jnp.bfloat16
ROWS, COLS, GROUPS, SUB, LANES = 64, 512, 8, 8, 128
HALF = LANES // 2
RADIUS = 4
UNROLL = 16
SCALE = -4.0 * 1.4426950408889634


def lane_ids(shape):
    return lax.broadcasted_iota(jnp.int32, shape, len(shape) - 1)


def split3(x):
    hi = x.astype(BF16)
    rest = x - hi.astype(F32)
    mid = rest.astype(BF16)
    low = (rest - mid.astype(F32)).astype(BF16)
    return jnp.concatenate([hi, mid, low], axis=0)


def permuted(x, perm, transposed):
    n = x.shape[0]
    dims = (((1,), (1 if transposed else 0,)), ((), ()))
    out = lax.dot_general(split3(x), perm, dims, preferred_element_type=F32)
    return out[:n] + out[n : 2 * n] + out[2 * n :]


def fill_perm(perm_ref):
    for k in range(4):
        shape = (128, COLS)
        n = lax.broadcasted_iota(jnp.int32, shape, 1)
        c = lax.broadcasted_iota(jnp.int32, shape, 0) + 128 * k
        hit = c == 8 * (n & 63) + (n >> 6)
        perm_ref[pl.ds(128 * k, 128), :] = jnp.where(hit, 1.0, 0.0).astype(BF16)


def spread(x, perm):
    y = permuted(x, perm, False)
    low = lane_ids((x.shape[0], LANES)) < HALF
    out = []
    for k in range(4):
        v = y[:, LANES * k : LANES * (k + 1)]
        w = pltpu.roll(v, HALF, 1)
        out += [jnp.where(low, v, w), jnp.where(low, w, v)]
    return out


def row_box(x):
    shape = x[0].shape
    pos = lane_ids(shape) & (HALF - 1)
    first, last = pos == 0, pos == HALF - 1
    pre = [x[0]]
    for k in range(1, 8):
        pre.append(pre[-1] + x[k])
    suf = [None] * 8
    suf[7] = x[7]
    for k in range(6, 0, -1):
        suf[k] = suf[k + 1] + x[k]
    suf[0] = pre[7]
    out = []
    for j in range(4):
        out.append(jnp.where(first, 0.0, pltpu.roll(suf[j + 4], 1, 1)) + pre[j + 4])
    for j in range(4, 8):
        out.append(jnp.where(last, 0.0, pltpu.roll(pre[j - 4], LANES - 1, 1)) + suf[j - 4])
    return out


def guide_fields(g, perm, pad_ref, g_ref, a1_ref, a2_ref, i4_ref, mg_ref, inv_ref):
    gd = spread(g, perm)
    zero = jnp.zeros((SUB, LANES), F32)
    for j in range(8):
        g_ref[j] = gd[j]
        for n, field in enumerate((gd[j], gd[j] * gd[j])):
            at = 2 * j + n
            pad_ref[at, pl.ds(0, SUB), :] = zero
            pad_ref[at, pl.ds(SUB, ROWS), :] = field
            pad_ref[at, pl.ds(SUB + ROWS, SUB), :] = zero

    def tile(i, carry):
        base = pl.multiple_of(i * SUB, SUB)
        sums = []
        for at in range(16):
            total = pad_ref[at, pl.ds(base + SUB - RADIUS, SUB), :]
            for k in range(1, 2 * RADIUS + 1):
                total = total + pad_ref[at, pl.ds(base + SUB - RADIUS + k, SUB), :]
            sums.append(total)
        bg, bgg = row_box(sums[0::2]), row_box(sums[1::2])
        shape = (SUB, LANES)
        r = lax.broadcasted_iota(jnp.int32, shape, 0) + base
        nr = jnp.minimum(r + RADIUS, ROWS - 1) - jnp.maximum(r - RADIUS, 0) + 1
        l8 = 8 * (lane_ids(shape) & (HALF - 1))
        for j in range(8):
            c = l8 + j
            nc = jnp.minimum(c + RADIUS, COLS - 1) - jnp.maximum(c - RADIUS, 0) + 1
            inv = 1.0 / (nr * nc).astype(F32)
            mean = bg[j] * inv
            var = bgg[j] * inv - mean * mean
            a1 = (SCALE * inv) / (var + 50.0)
            here = pl.ds(base, SUB)
            a1_ref[j, here, :] = a1
            a2_ref[j, here, :] = a1 * mean
            i4_ref[j, here, :] = SCALE * inv
            mg_ref[j, here, :] = mean
            inv_ref[j, here, :] = inv
        return carry

    lax.fori_loop(0, ROWS // SUB, tile, 0)


def forward_table(f, shift, perm, z_ref):
    base = spread(pltpu.roll(f, COLS - shift, 1), perm)
    low = lane_ids((ROWS, LANES)) < HALF
    for e in range(8):
        one = pltpu.roll(base[e], LANES - 1, 1)
        two = pltpu.roll(one, LANES - 1, 1)
        z_ref[pl.ds(e, ROWS, stride=16), :] = jnp.where(low, base[e], one)
        z_ref[pl.ds(e + 8, ROWS, stride=16), :] = jnp.where(low, one, two)


def side_table(s, shift, perm, y_ref, pad_ref):
    base = spread(pltpu.roll(s, ROWS - shift, 0), perm)
    low = lane_ids((SUB, LANES)) < HALF
    for j in range(8):
        tiles = [base[j][SUB * k : SUB * (k + 1)] for k in range(8)]
        for k in range(9):
            y_ref[j, pl.ds(SUB * k, SUB), :] = jnp.where(low, tiles[k % 8], tiles[(k + 1) % 8])


def bcast(ref, j, r):
    return jnp.broadcast_to(ref[j, pl.ds(r, 1), :], (SUB, LANES))


def cost_pass(load, g_ref, hx_ref, hy_ref):
    def row(r, carry):
        xs, ys = [], []
        for j in range(8):
            g = bcast(g_ref, j, r)
            x = jnp.abs(g - load(r, j))
            xs.append(x)
            ys.append(g * x)
        for ref, vals in ((hx_ref, xs), (hy_ref, ys)):
            for j, v in enumerate(row_box(vals)):
                ref[j, r] = v
        return carry

    lax.fori_loop(0, ROWS, row, 0, unroll=UNROLL)


def coef_pass(hx_ref, hy_ref, wa_ref, wb_ref, a1_ref, a2_ref, i4_ref, mg_ref):
    def column(j, carry):
        def window(ref):
            total = ref[j, 0]
            for r in range(1, RADIUS):
                total = total + ref[j, r]
            return total

        p, q = window(hx_ref), window(hy_ref)
        olda, oldb = [], []
        wa = wb = None
        for r in range(ROWS + RADIUS):
            if r < ROWS:
                if r + RADIUS < ROWS:
                    if r > RADIUS:
                        p = p + (hx_ref[j, r + RADIUS] - hx_ref[j, r - RADIUS - 1])
                        q = q + (hy_ref[j, r + RADIUS] - hy_ref[j, r - RADIUS - 1])
                    else:
                        p = p + hx_ref[j, r + RADIUS]
                        q = q + hy_ref[j, r + RADIUS]
                else:
                    p = p - hx_ref[j, r - RADIUS - 1]
                    q = q - hy_ref[j, r - RADIUS - 1]
                ca = q * bcast(a1_ref, j, r) - p * bcast(a2_ref, j, r)
                cb = p * bcast(i4_ref, j, r) - ca * bcast(mg_ref, j, r)
                olda.append(ca)
                oldb.append(cb)
                if r == 0:
                    wa, wb = ca, cb
                elif r > 2 * RADIUS:
                    wa = wa + (ca - olda[r - 2 * RADIUS - 1])
                    wb = wb + (cb - oldb[r - 2 * RADIUS - 1])
                else:
                    wa, wb = wa + ca, wb + cb
            else:
                wa = wa - olda[r - 2 * RADIUS - 1]
                wb = wb - oldb[r - 2 * RADIUS - 1]
            if r >= RADIUS:
                wa_ref[j, r - RADIUS] = wa
                wb_ref[j, r - RADIUS] = wb
        return carry

    lax.fori_loop(0, 8, column, 0)


def score_pass(start, rows, wa_ref, wb_ref, g_ref, inv_ref, sc_ref):
    def row(i, carry):
        r = start + i
        ha = row_box([wa_ref[j, r] for j in range(8)])
        hb = row_box([wb_ref[j, r] for j in range(8)])
        for j in range(8):
            sc_ref[r, pl.ds(SUB * j, SUB), :] = (ha[j] * bcast(g_ref, j, r) + hb[j]) * bcast(inv_ref, j, r)
        return carry

    lax.fori_loop(0, rows, row, 0, unroll=min(UNROLL, rows))


def softmax_pass(start, rows, sc_ref, d_ref, c_ref):
    def row(i, carry):
        r = start + i
        high = lane_ids((SUB, LANES)) >= HALF
        t = [sc_ref[r, pl.ds(s, SUB, stride=SUB), :] for s in range(8)]
        top = t[0]
        for s in range(1, 8):
            top = jnp.maximum(top, t[s])
        top = jnp.maximum(top, pltpu.roll(top, HALF, 1))
        total = lift = square = None
        for s in range(7, -1, -1):
            w = jnp.exp2(t[s] - top)
            total = w if total is None else total + w
            square = w * w if square is None else square + w * w
            if s:
                lift = total if lift is None else lift + total
        lift = lift + jnp.where(high, 8.0 * total, 0.0)
        total = total + pltpu.roll(total, HALF, 1)
        lift = lift + pltpu.roll(lift, HALF, 1)
        square = square + pltpu.roll(square, HALF, 1)
        unit = 1.0 / total
        d_ref[pl.ds(pl.multiple_of(r * SUB, SUB), SUB), :] = lift * unit
        c_ref[pl.ds(pl.multiple_of(r * SUB, SUB), SUB), :] = square * unit * unit
        return carry

    lax.fori_loop(0, rows, row, 0, unroll=min(UNROLL, rows))


def gathered(start, rows, refs, perm):
    low = lane_ids((rows, LANES)) < HALF
    stacked = []
    for ref in refs:
        parts = []
        for k in range(4):
            even = ref[pl.ds(SUB * start + 2 * k, rows, stride=SUB), :]
            odd = ref[pl.ds(SUB * start + 2 * k + 1, rows, stride=SUB), :]
            parts.append(jnp.where(low, even, odd))
        stacked.append(jnp.concatenate(parts, axis=1))
    return permuted(jnp.concatenate(stacked, axis=0), perm, True)


SCRATCH = dict(
    perm=((COLS, COLS), BF16), pad=((16, ROWS + 16, LANES), F32),
    g=((8, ROWS, LANES), F32), a1=((8, ROWS, LANES), F32), a2=((8, ROWS, LANES), F32),
    i4=((8, ROWS, LANES), F32), mg=((8, ROWS, LANES), F32), inv=((8, ROWS, LANES), F32),
    z=((16 * ROWS, LANES), F32), y=((8, ROWS + SUB, LANES), F32),
    hx=((8, ROWS, SUB, LANES), F32), hy=((8, ROWS, SUB, LANES), F32),
    wa=((8, ROWS, SUB, LANES), F32), wb=((8, ROWS, SUB, LANES), F32),
    sc=((ROWS, SUB * SUB, LANES), F32), d=((ROWS * SUB, LANES), F32), c=((ROWS * SUB, LANES), F32),
)


def load_forward(b):
    return lambda r, j: b["z"][pl.ds(r * 16 + j, SUB), :]


def load_side(b):
    return lambda r, j: b["y"][j, pl.ds(r, SUB), :]


MESH = pl.DeviceIdType.MESH


def kernel(chunks, t_ref, images_ref, out_ref, *refs):
    names = list(SCRATCH)
    b = dict(zip(names, refs))
    own, f_in, s_in, stage, zeros, here, put, sent, got, copied = refs[len(names) :]
    perm = b["perm"]
    axes = {"along": (lax.axis_index("along"), lax.axis_size("along")), "strip": (lax.axis_index("strip"), lax.axis_size("strip"))}

    barrier = pltpu.get_barrier_semaphore()
    for axis, (at, count) in axes.items():
        for step in (1, count - 1):
            pl.semaphore_signal(barrier, inc=1, device_id={axis: lax.rem(at + step, count)}, device_id_type=MESH)
    load_own = pltpu.make_async_copy(images_ref, own, here)
    load_own.start()
    pl.semaphore_wait(barrier, 4)

    def send(axis, step, src, dst, slot):
        at, _ = axes[axis]
        return pltpu.make_async_remote_copy(
            src_ref=src, dst_ref=dst, send_sem=sent.at[slot], recv_sem=got.at[slot],
            device_id={axis: at + step}, device_id_type=MESH)

    plan = (("along", f_in, 0, 0), ("strip", s_in, 1, 4))
    image_copies = []
    for axis, landing, slot, _ in plan:
        at, count = axes[axis]
        copy = send(axis, -1, images_ref, landing, slot)
        image_copies.append(copy)

        @pl.when(at > 0)
        def _():
            copy.start()

        @pl.when(at == count - 1)
        def _():
            landing[...] = jnp.zeros_like(landing)

    zeros[...] = jnp.zeros_like(zeros)
    fill_perm(perm)
    load_own.wait()
    guide_fields(own[...], perm[...], b["pad"], b["g"], b["a1"], b["a2"], b["i4"], b["mg"], b["inv"])

    slot = 2
    waits, local = [], []
    for which, (axis, landing, _, base) in enumerate(plan):
        at, count = axes[axis]
        image_copy = image_copies[which]
        empty = pltpu.make_async_copy(zeros, out_ref.at[pl.ds(base + 2, 2)], copied.at[which])

        @pl.when(at == 0)
        def _():
            empty.start()

        @pl.when(at < count - 1)
        def _():
            image_copy.wait_recv()

        if which == 0:
            forward_table(landing[...], t_ref[0], perm[...], b["z"])
            load = load_forward(b)
        else:
            side_table(landing[...], t_ref[1], perm[...], b["y"], b["pad"])
            load = load_side(b)
        cost_pass(load, b["g"], b["hx"], b["hy"])
        coef_pass(b["hx"], b["hy"], b["wa"], b["wb"], b["a1"], b["a2"], b["i4"], b["mg"])
        rows = ROWS // chunks[which]
        for chunk in range(chunks[which]):
            start = chunk * rows
            score_pass(start, rows, b["wa"], b["wb"], b["g"], b["inv"], b["sc"])
            softmax_pass(start, rows, b["sc"], b["d"], b["c"])
            both = gathered(start, rows, (b["d"], b["c"]), perm[...])
            span = pl.ds(start, rows)
            stage[which, 0, span, :] = both[:rows]
            stage[which, 1, span, :] = both[rows:]
            source = stage.at[which, :, span, :]
            mine = pltpu.make_async_copy(source, out_ref.at[pl.ds(base, 2), span, :], put.at[slot - 2])
            mine.start()
            local.append(mine)
            copy = send(axis, 1, source, out_ref.at[pl.ds(base + 2, 2), span, :], slot)

            @pl.when(at < count - 1)
            def _():
                copy.start()

            waits.append((at, count, copy))
            slot += 1

    for which, (axis, _, _, base) in enumerate(plan):
        at, count = axes[axis]
        image_copy = image_copies[which]
        empty = pltpu.make_async_copy(zeros, out_ref.at[pl.ds(base + 2, 2)], copied.at[which])

        @pl.when(at > 0)
        def _():
            image_copy.wait_send()

        @pl.when(at == 0)
        def _():
            empty.wait()

    for mine in local:
        mine.wait()
    for at, count, copy in waits:

        @pl.when(at < count - 1)
        def _():
            copy.wait_send()

        @pl.when(at > 0)
        def _():
            copy.wait_recv()


CHUNKS = (2, 4)


def per_device(images, offsets):
    pieces = sum(CHUNKS)
    return pl.pallas_call(
        functools.partial(kernel, CHUNKS),
        out_shape=jax.ShapeDtypeStruct((8, ROWS, COLS), F32),
        in_specs=[pl.BlockSpec(memory_space=pltpu.SMEM), pl.BlockSpec(memory_space=pl.ANY)],
        out_specs=pl.BlockSpec(memory_space=pl.ANY),
        scratch_shapes=[pltpu.VMEM(*v) for v in SCRATCH.values()]
        + [pltpu.VMEM((ROWS, COLS), F32)] * 3
        + [pltpu.VMEM((2, 2, ROWS, COLS), F32), pltpu.VMEM((2, ROWS, COLS), F32)]
        + [
            pltpu.SemaphoreType.DMA,
            pltpu.SemaphoreType.DMA((pieces,)),
            pltpu.SemaphoreType.DMA((2 + pieces,)),
            pltpu.SemaphoreType.DMA((2 + pieces,)),
            pltpu.SemaphoreType.DMA((2,)),
        ],
        compiler_params=pltpu.CompilerParams(collective_id=0, has_side_effects=True, vmem_limit_bytes=48 << 20),
    )(offsets.reshape(2), images)


def solution(mesh):
    placed = (P("strip", "along"), P("strip", "along", None))
    return jax.shard_map(
        per_device, mesh=mesh, in_specs=placed, out_specs=P(None, "strip", "along"), check_vma=False
    )
```

```python
import functools
import jax
import jax.numpy as jnp
from jax import lax
from jax.experimental import pallas as pl
from jax.experimental.pallas import tpu as pltpu
from jax.sharding import PartitionSpec as P

F32 = jnp.float32
BF16 = jnp.bfloat16
ROWS, COLS, GROUPS, SUB, LANES = 64, 512, 8, 8, 128
HALF = LANES // 2
RADIUS = 4
UNROLL = 16
COST_UNROLL = 16
SCALE = -4.0 * 1.4426950408889634


def lane_ids(shape):
    return lax.broadcasted_iota(jnp.int32, shape, len(shape) - 1)


def split3(x):
    hi = x.astype(BF16)
    rest = x - hi.astype(F32)
    mid = rest.astype(BF16)
    low = (rest - mid.astype(F32)).astype(BF16)
    return jnp.concatenate([hi, mid, low], axis=0)


def permuted(x, perm, transposed):
    n = x.shape[0]
    dims = (((1,), (1 if transposed else 0,)), ((), ()))
    out = lax.dot_general(split3(x), perm, dims, preferred_element_type=F32)
    return out[:n] + out[n : 2 * n] + out[2 * n :]


def fill_perm(perm_ref):
    for k in range(4):
        shape = (128, COLS)
        n = lax.broadcasted_iota(jnp.int32, shape, 1)
        c = lax.broadcasted_iota(jnp.int32, shape, 0) + 128 * k
        hit = c == 8 * (n & 63) + (n >> 6)
        perm_ref[pl.ds(128 * k, 128), :] = jnp.where(hit, 1.0, 0.0).astype(BF16)


def spread(x, perm):
    y = permuted(x, perm, False)
    low = lane_ids((x.shape[0], LANES)) < HALF
    out = []
    for k in range(4):
        v = y[:, LANES * k : LANES * (k + 1)]
        w = pltpu.roll(v, HALF, 1)
        out += [jnp.where(low, v, w), jnp.where(low, w, v)]
    return out


def row_box(x):
    shape = x[0].shape
    pos = lane_ids(shape) & (HALF - 1)
    first, last = pos == 0, pos == HALF - 1
    pre = [x[0]]
    for k in range(1, 8):
        pre.append(pre[-1] + x[k])
    suf = [None] * 8
    suf[7] = x[7]
    for k in range(6, 0, -1):
        suf[k] = suf[k + 1] + x[k]
    suf[0] = pre[7]
    out = []
    for j in range(4):
        out.append(jnp.where(first, 0.0, pltpu.roll(suf[j + 4], 1, 1)) + pre[j + 4])
    for j in range(4, 8):
        out.append(jnp.where(last, 0.0, pltpu.roll(pre[j - 4], LANES - 1, 1)) + suf[j - 4])
    return out


def guide_fields(g, perm, pad_ref, g_ref, a1_ref, a2_ref, i4_ref, mg_ref, inv_ref):
    gd = spread(g, perm)
    for j, v in enumerate(widened(gd)):
        g_ref[j] = v
    zero = jnp.zeros((SUB, LANES), F32)
    for j in range(8):
        for n, field in enumerate((gd[j], gd[j] * gd[j])):
            at = 2 * j + n
            pad_ref[at, pl.ds(0, SUB), :] = zero
            pad_ref[at, pl.ds(SUB, ROWS), :] = field
            pad_ref[at, pl.ds(SUB + ROWS, SUB), :] = zero

    def tile(i, carry):
        base = pl.multiple_of(i * SUB, SUB)
        sums = []
        for at in range(16):
            total = pad_ref[at, pl.ds(base + SUB - RADIUS, SUB), :]
            for k in range(1, 2 * RADIUS + 1):
                total = total + pad_ref[at, pl.ds(base + SUB - RADIUS + k, SUB), :]
            sums.append(total)
        bg, bgg = row_box(sums[0::2]), row_box(sums[1::2])
        shape = (SUB, LANES)
        r = lax.broadcasted_iota(jnp.int32, shape, 0) + base
        nr = jnp.minimum(r + RADIUS, ROWS - 1) - jnp.maximum(r - RADIUS, 0) + 1
        l8 = 8 * (lane_ids(shape) & (HALF - 1))
        for j in range(8):
            c = l8 + j
            nc = jnp.minimum(c + RADIUS, COLS - 1) - jnp.maximum(c - RADIUS, 0) + 1
            inv = 1.0 / (nr * nc).astype(F32)
            mean = bg[j] * inv
            var = bgg[j] * inv - mean * mean
            a1 = (SCALE * inv) / (var + 50.0)
            here = pl.ds(base, SUB)
            a1_ref[j, here, :] = a1
            a2_ref[j, here, :] = a1 * mean
            i4_ref[j, here, :] = SCALE * inv
            mg_ref[j, here, :] = mean
            inv_ref[j, here, :] = inv
        return carry

    lax.fori_loop(0, ROWS // SUB, tile, 0)


def ends(shape):
    pos = lane_ids(shape) & (HALF - 1)
    return pos == 0, pos == HALF - 1


def widened(x):
    first, last = ends(x[0].shape)
    before = [jnp.where(first, 0.0, pltpu.roll(v, 1, 1)) for v in x[4:]]
    after = [jnp.where(last, 0.0, pltpu.roll(v, LANES - 1, 1)) for v in x[:4]]
    return before + list(x) + after


STEP = 24


def forward_table(f, shift, perm, z_ref):
    base = spread(pltpu.roll(f, COLS - shift, 1), perm)
    low = lane_ids((ROWS, LANES)) < HALF
    turned = {(k, 0): base[k] for k in range(8)}
    for k in range(8):
        for q in ((-1,) if k >= 4 else ()) + (1, 2) + ((3,) if k < 3 else ()):
            turned[k, q] = pltpu.roll(base[k], (-q) % LANES, 1)
    for e in range(-4, 19):
        q, k = divmod(e, 8)
        z_ref[pl.ds(e + 4, ROWS, stride=STEP), :] = jnp.where(low, turned[k, q], turned[k, q + 1])


def side_table(s, shift, perm, y_ref):
    base = widened(spread(pltpu.roll(s, ROWS - shift, 0), perm))
    low = lane_ids((SUB, LANES)) < HALF
    for j in range(16):
        tiles = [base[j][SUB * k : SUB * (k + 1)] for k in range(8)]
        for k in range(9):
            y_ref[j, pl.ds(SUB * k, SUB), :] = jnp.where(low, tiles[k % 8], tiles[(k + 1) % 8])


def bcast(ref, j, r):
    return jnp.broadcast_to(ref[j, pl.ds(r, 1), :], (SUB, LANES))


def wide_box(x):
    suf = [x[7]]
    for k in range(6, -1, -1):
        suf.append(suf[-1] + x[k])
    suf.reverse()
    pre = [x[8]]
    for k in range(9, 16):
        pre.append(pre[-1] + x[k])
    return [suf[j] + pre[j] for j in range(8)]


def cost_pass(load, masked, g_ref, hx_ref, hy_ref):
    def row(r, carry):
        first, last = ends((SUB, LANES))
        xs, ys = [], []
        for j in range(16):
            g = bcast(g_ref, j, r)
            x = jnp.abs(g - load(r, j))
            if masked and j < 4:
                x = jnp.where(first, 0.0, x)
            if masked and j >= 12:
                x = jnp.where(last, 0.0, x)
            xs.append(x)
            ys.append(g * x)
        for ref, vals in ((hx_ref, xs), (hy_ref, ys)):
            for j, v in enumerate(wide_box(vals)):
                ref[j, r] = v
        return carry

    lax.fori_loop(0, ROWS, row, 0, unroll=COST_UNROLL)


def coef_pass(hx_ref, hy_ref, wa_ref, wb_ref, a1_ref, a2_ref, i4_ref, mg_ref):
    def column(j, carry):
        def window(ref):
            total = ref[j, 0]
            for r in range(1, RADIUS):
                total = total + ref[j, r]
            return total

        p, q = window(hx_ref), window(hy_ref)
        olda, oldb = [], []
        wa = wb = None
        for r in range(ROWS + RADIUS):
            if r < ROWS:
                if r + RADIUS < ROWS:
                    if r > RADIUS:
                        p = p + (hx_ref[j, r + RADIUS] - hx_ref[j, r - RADIUS - 1])
                        q = q + (hy_ref[j, r + RADIUS] - hy_ref[j, r - RADIUS - 1])
                    else:
                        p = p + hx_ref[j, r + RADIUS]
                        q = q + hy_ref[j, r + RADIUS]
                else:
                    p = p - hx_ref[j, r - RADIUS - 1]
                    q = q - hy_ref[j, r - RADIUS - 1]
                ca = q * bcast(a1_ref, j, r) - p * bcast(a2_ref, j, r)
                cb = p * bcast(i4_ref, j, r) - ca * bcast(mg_ref, j, r)
                olda.append(ca)
                oldb.append(cb)
                if r == 0:
                    wa, wb = ca, cb
                elif r > 2 * RADIUS:
                    wa = wa + (ca - olda[r - 2 * RADIUS - 1])
                    wb = wb + (cb - oldb[r - 2 * RADIUS - 1])
                else:
                    wa, wb = wa + ca, wb + cb
            else:
                wa = wa - olda[r - 2 * RADIUS - 1]
                wb = wb - oldb[r - 2 * RADIUS - 1]
            if r >= RADIUS:
                wa_ref[j, r - RADIUS] = wa
                wb_ref[j, r - RADIUS] = wb
        return carry

    lax.fori_loop(0, 8, column, 0)


def score_pass(start, rows, wa_ref, wb_ref, g_ref, inv_ref, sc_ref):
    def row(i, carry):
        r = start + i
        ha = row_box([wa_ref[j, r] for j in range(8)])
        hb = row_box([wb_ref[j, r] for j in range(8)])
        for j in range(8):
            sc_ref[r, pl.ds(SUB * j, SUB), :] = (ha[j] * bcast(g_ref, j + 4, r) + hb[j]) * bcast(inv_ref, j, r)
        return carry

    lax.fori_loop(0, rows, row, 0, unroll=min(32, rows))


def softmax_pass(start, rows, sc_ref, d_ref, c_ref):
    def row(i, carry):
        r = start + i
        high = lane_ids((SUB, LANES)) >= HALF
        t = [sc_ref[r, pl.ds(s, SUB, stride=SUB), :] for s in range(8)]
        top = t[0]
        for s in range(1, 8):
            top = jnp.maximum(top, t[s])
        top = jnp.maximum(top, pltpu.roll(top, HALF, 1))
        total = lift = square = None
        for s in range(7, -1, -1):
            w = jnp.exp2(t[s] - top)
            total = w if total is None else total + w
            square = w * w if square is None else square + w * w
            if s:
                lift = total if lift is None else lift + total
        lift = lift + jnp.where(high, 8.0 * total, 0.0)
        total = total + pltpu.roll(total, HALF, 1)
        lift = lift + pltpu.roll(lift, HALF, 1)
        square = square + pltpu.roll(square, HALF, 1)
        unit = 1.0 / total
        d_ref[pl.ds(pl.multiple_of(r * SUB, SUB), SUB), :] = lift * unit
        c_ref[pl.ds(pl.multiple_of(r * SUB, SUB), SUB), :] = square * unit * unit
        return carry

    lax.fori_loop(0, rows, row, 0, unroll=min(UNROLL, rows))


def gathered(start, rows, refs, perm):
    low = lane_ids((rows, LANES)) < HALF
    stacked = []
    for ref in refs:
        parts = []
        for k in range(4):
            even = ref[pl.ds(SUB * start + 2 * k, rows, stride=SUB), :]
            odd = ref[pl.ds(SUB * start + 2 * k + 1, rows, stride=SUB), :]
            parts.append(jnp.where(low, even, odd))
        stacked.append(jnp.concatenate(parts, axis=1))
    return permuted(jnp.concatenate(stacked, axis=0), perm, True)


SCRATCH = dict(
    perm=((COLS, COLS), BF16), pad=((16, ROWS + 16, LANES), F32),
    g=((16, ROWS, LANES), F32), a1=((8, ROWS, LANES), F32), a2=((8, ROWS, LANES), F32),
    i4=((8, ROWS, LANES), F32), mg=((16, ROWS, LANES), F32), inv=((8, ROWS, LANES), F32),
    z=((24 * ROWS, LANES), F32), y=((16, ROWS + SUB, LANES), F32),
    hx=((8, ROWS, SUB, LANES), F32), hy=((8, ROWS, SUB, LANES), F32),
    wa=((8, ROWS, SUB, LANES), F32), wb=((8, ROWS, SUB, LANES), F32),
    sc=((ROWS, SUB * SUB, LANES), F32), d=((ROWS * SUB, LANES), F32), c=((ROWS * SUB, LANES), F32),
)


def load_forward(b):
    return lambda r, j: b["z"][pl.ds(r * STEP + j, SUB), :]


def load_side(b):
    return lambda r, j: b["y"][j, pl.ds(r, SUB), :]


MESH = pl.DeviceIdType.MESH
CHUNKS = (2, 4)


def kernel(offsets_ref, images_ref, out_ref, *refs):
    names = list(SCRATCH)
    b = dict(zip(names, refs))
    own, f_in, s_in, shifts, here, sent, got = refs[len(names) :]
    perm = b["perm"]
    axes = {name: (lax.axis_index(name), lax.axis_size(name)) for name in ("along", "strip")}

    barrier = pltpu.get_barrier_semaphore()
    ready = 0
    for axis, (at, count) in axes.items():
        for step in (1, -1):
            inside = jnp.logical_and(at + step >= 0, at + step < count)
            ready = ready + inside.astype(jnp.int32)

            @pl.when(inside)
            def _():
                pl.semaphore_signal(barrier, inc=1, device_id={axis: at + step}, device_id_type=MESH)

    load_own = pltpu.make_async_copy(images_ref, own, here.at[0])
    load_own.start()
    load_shifts = pltpu.make_async_copy(offsets_ref, shifts, here.at[1])
    load_shifts.start()
    fill_perm(perm)
    plan = (("along", f_in, 0), ("strip", s_in, 4))
    for axis, landing, base in plan:
        at, count = axes[axis]

        @pl.when(at == count - 1)
        def _():
            landing[...] = jnp.zeros_like(landing)

        @pl.when(at == 0)
        def _():
            out_ref[pl.ds(base + 2, 2)] = jnp.zeros((2, ROWS, COLS), F32)

    pl.semaphore_wait(barrier, ready)

    def send(axis, step, src, dst, slot):
        at, _ = axes[axis]
        return pltpu.make_async_remote_copy(
            src_ref=src, dst_ref=dst, send_sem=sent.at[slot], recv_sem=got.at[slot],
            device_id={axis: at + step}, device_id_type=MESH)

    image_copies = [send(axis, -1, images_ref, landing, slot) for slot, (axis, landing, _) in enumerate(plan)]

    def start_image(which, also=True):
        at, _ = axes[plan[which][0]]
        pl.when(jnp.logical_and(at > 0, also))(image_copies[which].start)

    def await_image(which):
        at, count = axes[plan[which][0]]
        pl.when(at < count - 1)(image_copies[which].wait_recv)

    near = lax.rem(axes["along"][0], 2) == 1
    start_image(0)
    start_image(1, near)
    load_own.wait()
    load_shifts.wait()
    guide_fields(own[...], perm[...], b["pad"], b["g"], b["a1"], b["a2"], b["i4"], b["mg"], b["inv"])
    pl.when(axes["along"][0] > 0)(image_copies[0].wait_send)
    start_image(1, jnp.logical_not(near))
    await_image(0)

    slot = 2
    waits = []
    for which, (axis, landing, base) in enumerate(plan):
        at, count = axes[axis]
        if which == 0:
            forward_table(landing[...], shifts[0, 0, 0], perm[...], b["z"])
            load = load_forward(b)
        else:
            await_image(1)
            side_table(landing[...], shifts[0, 0, 1], perm[...], b["y"])
            load = load_side(b)
        cost_pass(load, which == 0, b["g"], b["hx"], b["hy"])
        coef_pass(b["hx"], b["hy"], b["wa"], b["wb"], b["a1"], b["a2"], b["i4"], b["mg"])
        rows = ROWS // CHUNKS[which]
        for chunk in range(CHUNKS[which]):
            start = chunk * rows
            score_pass(start, rows, b["wa"], b["wb"], b["g"], b["inv"], b["sc"])
            softmax_pass(start, rows, b["sc"], b["d"], b["c"])
            both = gathered(start, rows, (b["d"], b["c"]), perm[...])
            span = pl.ds(start, rows)
            out_ref[base, span, :] = both[:rows]
            out_ref[base + 1, span, :] = both[rows:]
            copy = send(axis, 1, out_ref.at[pl.ds(base, 2), span, :], out_ref.at[pl.ds(base + 2, 2), span, :], slot)
            pl.when(at < count - 1)(copy.start)
            waits.append((at, count, copy))
            slot += 1

    pl.when(axes["strip"][0] > 0)(image_copies[1].wait_send)
    for at, count, copy in waits:
        pl.when(at < count - 1)(copy.wait_send)
        pl.when(at > 0)(copy.wait_recv)


def per_device(images, offsets):
    slots = 2 + sum(CHUNKS)
    return pl.pallas_call(
        kernel,
        out_shape=jax.ShapeDtypeStruct((8, ROWS, COLS), F32),
        in_specs=[pl.BlockSpec(memory_space=pltpu.HBM), pl.BlockSpec(memory_space=pltpu.HBM)],
        out_specs=pl.BlockSpec(memory_space=pltpu.VMEM),
        scratch_shapes=[pltpu.VMEM(*v) for v in SCRATCH.values()]
        + [pltpu.VMEM((ROWS, COLS), F32)] * 3
        + [
            pltpu.SMEM((1, 1, 2), jnp.int32),
            pltpu.SemaphoreType.DMA((2,)),
            pltpu.SemaphoreType.DMA((slots,)),
            pltpu.SemaphoreType.DMA((slots,)),
        ],
        compiler_params=pltpu.CompilerParams(collective_id=0, has_side_effects=True, vmem_limit_bytes=48 << 20),
    )(pltpu.with_memory_space_constraint(offsets, pltpu.HBM), pltpu.with_memory_space_constraint(images, pltpu.HBM))


def solution(mesh):
    placed = (P("strip", "along"), P("strip", "along", None))
    return jax.shard_map(
        per_device, mesh=mesh, in_specs=placed, out_specs=P(None, "strip", "along"), check_vma=False
    )
```

```python
import functools
import jax
import jax.numpy as jnp
from jax import lax
from jax.experimental import pallas as pl
from jax.experimental.pallas import tpu as pltpu
from jax.sharding import PartitionSpec as P

F32 = jnp.float32
BF16 = jnp.bfloat16
ROWS, COLS, GROUPS, SUB, LANES = 64, 512, 8, 8, 128
HALF = LANES // 2
RADIUS = 4
UNROLL = 16
COST_UNROLL = 16
SCALE = -4.0 * 1.4426950408889634


def lane_ids(shape):
    return lax.broadcasted_iota(jnp.int32, shape, len(shape) - 1)


def split3(x):
    hi = x.astype(BF16)
    rest = x - hi.astype(F32)
    mid = rest.astype(BF16)
    low = (rest - mid.astype(F32)).astype(BF16)
    return jnp.concatenate([hi, mid, low], axis=0)


def permuted(x, perm):
    n = x.shape[0]
    out = jnp.dot(split3(x), perm, preferred_element_type=F32)
    return out[:n] + out[n : 2 * n] + out[2 * n :]


def fill_perm(perm_ref, back_ref):
    for k in range(4):
        shape = (128, COLS)
        along = lax.broadcasted_iota(jnp.int32, shape, 1)
        down = lax.broadcasted_iota(jnp.int32, shape, 0) + 128 * k
        rows = pl.ds(128 * k, 128)
        perm_ref[rows, :] = jnp.where(down == 8 * (along & 63) + (along >> 6), 1.0, 0.0).astype(BF16)
        back_ref[rows, :] = jnp.where(along == 8 * (down & 63) + (down >> 6), 1.0, 0.0).astype(BF16)


def spread(x, perm):
    y = permuted(x, perm)
    low = lane_ids((x.shape[0], LANES)) < HALF
    out = []
    for k in range(4):
        v = y[:, LANES * k : LANES * (k + 1)]
        w = pltpu.roll(v, HALF, 1)
        out += [jnp.where(low, v, w), jnp.where(low, w, v)]
    return out


def row_box(x):
    shape = x[0].shape
    pos = lane_ids(shape) & (HALF - 1)
    first, last = pos == 0, pos == HALF - 1
    pre = [x[0]]
    for k in range(1, 8):
        pre.append(pre[-1] + x[k])
    suf = [None] * 8
    suf[7] = x[7]
    for k in range(6, 0, -1):
        suf[k] = suf[k + 1] + x[k]
    suf[0] = pre[7]
    out = []
    for j in range(4):
        out.append(jnp.where(first, 0.0, pltpu.roll(suf[j + 4], 1, 1)) + pre[j + 4])
    for j in range(4, 8):
        out.append(jnp.where(last, 0.0, pltpu.roll(pre[j - 4], LANES - 1, 1)) + suf[j - 4])
    return out


def guide_fields(g, perm, pad_ref, g_ref, a1_ref, a2_ref, i4_ref, mg_ref, inv_ref, then):
    gd = spread(g, perm)
    for j, v in enumerate(widened(gd)):
        g_ref[j] = v
    zero = jnp.zeros((SUB, LANES), F32)
    for j in range(8):
        for n, field in enumerate((gd[j], gd[j] * gd[j])):
            at = 2 * j + n
            pad_ref[at, pl.ds(0, SUB), :] = zero
            pad_ref[at, pl.ds(SUB, ROWS), :] = field
            pad_ref[at, pl.ds(SUB + ROWS, SUB), :] = zero

    then()

    def tile(i, carry):
        base = pl.multiple_of(i * SUB, SUB)
        sums = []
        for at in range(16):
            total = pad_ref[at, pl.ds(base + SUB - RADIUS, SUB), :]
            for k in range(1, 2 * RADIUS + 1):
                total = total + pad_ref[at, pl.ds(base + SUB - RADIUS + k, SUB), :]
            sums.append(total)
        bg, bgg = row_box(sums[0::2]), row_box(sums[1::2])
        shape = (SUB, LANES)
        r = lax.broadcasted_iota(jnp.int32, shape, 0) + base
        nr = jnp.minimum(r + RADIUS, ROWS - 1) - jnp.maximum(r - RADIUS, 0) + 1
        l8 = 8 * (lane_ids(shape) & (HALF - 1))
        for j in range(8):
            c = l8 + j
            nc = jnp.minimum(c + RADIUS, COLS - 1) - jnp.maximum(c - RADIUS, 0) + 1
            inv = 1.0 / (nr * nc).astype(F32)
            mean = bg[j] * inv
            var = bgg[j] * inv - mean * mean
            a1 = (SCALE * inv) / (var + 50.0)
            here = pl.ds(base, SUB)
            a1_ref[j, here, :] = a1
            a2_ref[j, here, :] = a1 * mean
            i4_ref[j, here, :] = SCALE * inv
            mg_ref[j, here, :] = mean
            inv_ref[j, here, :] = inv
        return carry

    lax.fori_loop(0, ROWS // SUB, tile, 0)


def ends(shape):
    pos = lane_ids(shape) & (HALF - 1)
    return pos == 0, pos == HALF - 1


def widened(x):
    first, last = ends(x[0].shape)
    before = [jnp.where(first, 0.0, pltpu.roll(v, 1, 1)) for v in x[4:]]
    after = [jnp.where(last, 0.0, pltpu.roll(v, LANES - 1, 1)) for v in x[:4]]
    return before + list(x) + after


STEP = 24


def forward_table(f, shift, perm, z_ref):
    base = spread(pltpu.roll(f, COLS - shift, 1), perm)
    low = lane_ids((ROWS, LANES)) < HALF
    turned = {(k, 0): base[k] for k in range(8)}
    for k in range(8):
        for q in ((-1,) if k >= 4 else ()) + (1, 2) + ((3,) if k < 3 else ()):
            turned[k, q] = pltpu.roll(base[k], (-q) % LANES, 1)
    for e in range(-4, 19):
        q, k = divmod(e, 8)
        z_ref[pl.ds(e + 4, ROWS, stride=STEP), :] = jnp.where(low, turned[k, q], turned[k, q + 1])


def side_table(s, shift, perm, y_ref):
    base = widened(spread(pltpu.roll(s, ROWS - shift, 0), perm))
    low = lane_ids((SUB, LANES)) < HALF
    for j in range(16):
        tiles = [base[j][SUB * k : SUB * (k + 1)] for k in range(8)]
        for k in range(9):
            y_ref[j, pl.ds(SUB * k, SUB), :] = jnp.where(low, tiles[k % 8], tiles[(k + 1) % 8])


def bcast(ref, j, r):
    return jnp.broadcast_to(ref[j, pl.ds(r, 1), :], (SUB, LANES))


def wide_box(x):
    suf = [x[7]]
    for k in range(6, -1, -1):
        suf.append(suf[-1] + x[k])
    suf.reverse()
    pre = [x[8]]
    for k in range(9, 16):
        pre.append(pre[-1] + x[k])
    return [suf[j] + pre[j] for j in range(8)]


def cost_pass(load, masked, g_ref, hx_ref, hy_ref):
    def row(r, carry):
        first, last = ends((SUB, LANES))
        xs, ys = [], []
        for j in range(16):
            g = bcast(g_ref, j, r)
            x = jnp.abs(g - load(r, j))
            if masked and j < 4:
                x = jnp.where(first, 0.0, x)
            if masked and j >= 12:
                x = jnp.where(last, 0.0, x)
            xs.append(x)
            ys.append(g * x)
        for ref, vals in ((hx_ref, xs), (hy_ref, ys)):
            for j, v in enumerate(wide_box(vals)):
                ref[j, r] = v
        return carry

    lax.fori_loop(0, ROWS, row, 0, unroll=COST_UNROLL)


def coef_pass(hx_ref, hy_ref, wa_ref, wb_ref, a1_ref, a2_ref, i4_ref, mg_ref):
    def column(j, carry):
        def window(ref):
            total = ref[j, 0]
            for r in range(1, RADIUS):
                total = total + ref[j, r]
            return total

        p, q = window(hx_ref), window(hy_ref)
        olda, oldb = [], []
        wa = wb = None
        for r in range(ROWS + RADIUS):
            if r < ROWS:
                if r + RADIUS < ROWS:
                    if r > RADIUS:
                        p = p + (hx_ref[j, r + RADIUS] - hx_ref[j, r - RADIUS - 1])
                        q = q + (hy_ref[j, r + RADIUS] - hy_ref[j, r - RADIUS - 1])
                    else:
                        p = p + hx_ref[j, r + RADIUS]
                        q = q + hy_ref[j, r + RADIUS]
                else:
                    p = p - hx_ref[j, r - RADIUS - 1]
                    q = q - hy_ref[j, r - RADIUS - 1]
                ca = q * bcast(a1_ref, j, r) - p * bcast(a2_ref, j, r)
                cb = p * bcast(i4_ref, j, r) - ca * bcast(mg_ref, j, r)
                olda.append(ca)
                oldb.append(cb)
                if r == 0:
                    wa, wb = ca, cb
                elif r > 2 * RADIUS:
                    wa = wa + (ca - olda[r - 2 * RADIUS - 1])
                    wb = wb + (cb - oldb[r - 2 * RADIUS - 1])
                else:
                    wa, wb = wa + ca, wb + cb
            else:
                wa = wa - olda[r - 2 * RADIUS - 1]
                wb = wb - oldb[r - 2 * RADIUS - 1]
            if r >= RADIUS:
                wa_ref[j, r - RADIUS] = wa
                wb_ref[j, r - RADIUS] = wb
        return carry

    lax.fori_loop(0, 8, column, 0)


def running(x):
    head = [x[0]]
    for k in range(1, 8):
        head.append(head[-1] + x[k])
    tail = [head[7]] + [None] * 6 + [x[7]]
    for k in range(6, 0, -1):
        tail[k] = tail[k + 1] + x[k]
    return head, tail


def score_pass(start, rows, wa_ref, wb_ref, g_ref, inv_ref, sc_ref):
    def row(i, carry):
        r = start + i
        first, last = ends((SUB, LANES))
        ha, ta = running([wa_ref[j, r] for j in range(8)])
        hb, tb = running([wb_ref[j, r] for j in range(8)])
        for j in range(8):
            if j < 4:
                other = ta[j + 4] * bcast(g_ref, j + 12, r) + tb[j + 4]
                other = jnp.where(first, 0.0, pltpu.roll(other, 1, 1))
                same = ha[j + 4] * bcast(g_ref, j + 4, r) + hb[j + 4]
            else:
                other = ha[j - 4] * bcast(g_ref, j - 4, r) + hb[j - 4]
                other = jnp.where(last, 0.0, pltpu.roll(other, LANES - 1, 1))
                same = ta[j - 4] * bcast(g_ref, j + 4, r) + tb[j - 4]
            sc_ref[r, pl.ds(j, SUB, stride=SUB), :] = (same + other) * bcast(inv_ref, j, r)
        return carry

    lax.fori_loop(0, rows, row, 0, unroll=min(UNROLL, rows))


def softmax_pass(start, rows, sc_ref, d_ref, c_ref):
    def row(i, carry):
        r = start + i
        high = lane_ids((SUB, LANES)) >= HALF
        t = [sc_ref[r, pl.ds(SUB * s, SUB), :] for s in range(8)]
        top = t
        while len(top) > 1:
            top = [jnp.maximum(top[k], top[k + 1]) for k in range(0, len(top), 2)]
        top = jnp.maximum(top[0], pltpu.roll(top[0], HALF, 1))
        total = lift = square = None
        for s in range(7, -1, -1):
            w = jnp.exp2(t[s] - top)
            total = w if total is None else total + w
            square = w * w if square is None else square + w * w
            if s:
                lift = total if lift is None else lift + total
        lift = lift + jnp.where(high, 8.0 * total, 0.0)
        total = total + pltpu.roll(total, HALF, 1)
        lift = lift + pltpu.roll(lift, HALF, 1)
        square = square + pltpu.roll(square, HALF, 1)
        unit = 1.0 / total
        d_ref[pl.ds(pl.multiple_of(r * SUB, SUB), SUB), :] = lift * unit
        c_ref[pl.ds(pl.multiple_of(r * SUB, SUB), SUB), :] = square * unit * unit
        return carry

    lax.fori_loop(0, rows, row, 0, unroll=min(UNROLL, rows))


def gathered(start, rows, refs, perm):
    low = lane_ids((rows, LANES)) < HALF
    stacked = []
    for ref in refs:
        parts = []
        for k in range(4):
            even = ref[pl.ds(SUB * start + 2 * k, rows, stride=SUB), :]
            odd = ref[pl.ds(SUB * start + 2 * k + 1, rows, stride=SUB), :]
            parts.append(jnp.where(low, even, odd))
        stacked.append(jnp.concatenate(parts, axis=1))
    return permuted(jnp.concatenate(stacked, axis=0), perm)


SCRATCH = dict(
    perm=((COLS, COLS), BF16), back=((COLS, COLS), BF16), pad=((16, ROWS + 16, LANES), F32),
    g=((16, ROWS, LANES), F32), a1=((8, ROWS, LANES), F32), a2=((8, ROWS, LANES), F32),
    i4=((8, ROWS, LANES), F32), mg=((16, ROWS, LANES), F32), inv=((8, ROWS, LANES), F32),
    z=((24 * ROWS, LANES), F32), y=((16, ROWS + SUB, LANES), F32),
    hx=((8, ROWS, SUB, LANES), F32), hy=((8, ROWS, SUB, LANES), F32),
    wa=((8, ROWS, SUB, LANES), F32), wb=((8, ROWS, SUB, LANES), F32),
    sc=((ROWS, SUB * SUB, LANES), F32), d=((ROWS * SUB, LANES), F32), c=((ROWS * SUB, LANES), F32),
)


def load_forward(b):
    return lambda r, j: b["z"][pl.ds(r * STEP + j, SUB), :]


def load_side(b):
    return lambda r, j: b["y"][j, pl.ds(r, SUB), :]


MESH = pl.DeviceIdType.MESH
PIECES = 4


def kernel(offsets_ref, images_ref, out_ref, *refs):
    names = list(SCRATCH)
    b = dict(zip(names, refs))
    own, f_in, s_in, shifts, here, sent, got = refs[len(names) :]
    perm = b["perm"]
    axes = {name: (lax.axis_index(name), lax.axis_size(name)) for name in ("along", "strip")}

    barrier = pltpu.get_barrier_semaphore()
    for axis, (at, count) in axes.items():

        @pl.when(at < count - 1)
        def _():
            pl.semaphore_signal(barrier, inc=1, device_id={axis: at + 1}, device_id_type=MESH)

    load_own = pltpu.make_async_copy(images_ref, own, here.at[0])
    load_own.start()
    load_shifts = pltpu.make_async_copy(offsets_ref, shifts, here.at[1])
    load_shifts.start()
    fill_perm(perm, b["back"])
    plan = (("along", f_in, 0), ("strip", s_in, 4))
    for axis, landing, base in plan:
        at, count = axes[axis]

        @pl.when(at == count - 1)
        def _():
            landing[...] = jnp.zeros_like(landing)

        @pl.when(at == 0)
        def _():
            out_ref[pl.ds(base + 2, 2)] = jnp.zeros((2, ROWS, COLS), F32)

    ready = sum((at > 0).astype(jnp.int32) for at, _ in axes.values())

    @pl.when(ready > 0)
    def _():
        pl.semaphore_wait(barrier, ready)


    def send(axis, step, src, dst, slot):
        at, _ = axes[axis]
        return pltpu.make_async_remote_copy(
            src_ref=src, dst_ref=dst, send_sem=sent.at[slot], recv_sem=got.at[slot],
            device_id={axis: at + step}, device_id_type=MESH)

    image_copies = [send(axis, -1, images_ref, landing, slot) for slot, (axis, landing, _) in enumerate(plan)]

    def start_image(which, also=True):
        at, _ = axes[plan[which][0]]
        pl.when(jnp.logical_and(at > 0, also))(image_copies[which].start)

    def await_image(which):
        at, count = axes[plan[which][0]]
        pl.when(at < count - 1)(image_copies[which].wait_recv)

    odd = lax.rem(axes["along"][0], 2)
    start_image(0, odd == 1)
    start_image(1, odd == 1)
    load_own.wait()
    load_shifts.wait()
    guide_fields(own[...], perm[...], b["pad"], b["g"], b["a1"], b["a2"], b["i4"], b["mg"], b["inv"], lambda: start_image(0, odd == 0))
    rows = ROWS // PIECES

    def piece_copy(which, piece):
        axis, _, base = plan[which]
        span = pl.ds(pl.multiple_of(piece * rows, rows), rows)
        return send(
            axis, 1, out_ref.at[pl.ds(base, 2), span, :], out_ref.at[pl.ds(base + 2, 2), span, :],
            2 + which * PIECES + piece)

    def pair(step, carry):
        which = lax.rem(step + odd, 2)

        @pl.when(which == 0)
        def _():
            await_image(0)
            forward_table(f_in[...], shifts[0, 0, 0], perm[...], b["z"])
            start_image(1, odd == 0)
            cost_pass(load_forward(b), True, b["g"], b["hx"], b["hy"])

        @pl.when(which == 1)
        def _():
            await_image(1)
            side_table(s_in[...], shifts[0, 0, 1], perm[...], b["y"])
            cost_pass(load_side(b), False, b["g"], b["hx"], b["hy"])

        coef_pass(b["hx"], b["hy"], b["wa"], b["wb"], b["a1"], b["a2"], b["i4"], b["mg"])

        def piece_of(piece, inner):
            start = pl.multiple_of(piece * rows, rows)
            score_pass(start, rows, b["wa"], b["wb"], b["g"], b["inv"], b["sc"])
            softmax_pass(start, rows, b["sc"], b["d"], b["c"])
            both = gathered(start, rows, (b["d"], b["c"]), b["back"][...])
            span = pl.ds(start, rows)
            out_ref[4 * which, span, :] = both[:rows]
            out_ref[4 * which + 1, span, :] = both[rows:]
            for k, (axis, _, _) in enumerate(plan):
                at, count = axes[axis]
                pl.when(jnp.logical_and(which == k, at < count - 1))(piece_copy(k, piece).start)
            return inner

        lax.fori_loop(0, PIECES, piece_of, 0)
        return carry

    lax.fori_loop(0, 2, pair, 0)

    for which, (axis, _, _) in enumerate(plan):
        at, count = axes[axis]
        pl.when(at > 0)(image_copies[which].wait_send)
        for piece in range(PIECES):
            copy = piece_copy(which, piece)
            pl.when(at < count - 1)(copy.wait_send)
            pl.when(at > 0)(copy.wait_recv)


def per_device(images, offsets):
    slots = 2 + 2 * PIECES
    return pl.pallas_call(
        kernel,
        out_shape=jax.ShapeDtypeStruct((8, ROWS, COLS), F32),
        in_specs=[pl.BlockSpec(memory_space=pltpu.HBM), pl.BlockSpec(memory_space=pltpu.HBM)],
        out_specs=pl.BlockSpec(memory_space=pltpu.VMEM),
        scratch_shapes=[pltpu.VMEM(*v) for v in SCRATCH.values()]
        + [pltpu.VMEM((ROWS, COLS), F32)] * 3
        + [
            pltpu.SMEM((1, 1, 2), jnp.int32),
            pltpu.SemaphoreType.DMA((2,)),
            pltpu.SemaphoreType.DMA((slots,)),
            pltpu.SemaphoreType.DMA((slots,)),
        ],
        compiler_params=pltpu.CompilerParams(collective_id=0, has_side_effects=True, vmem_limit_bytes=48 << 20),
    )(pltpu.with_memory_space_constraint(offsets, pltpu.HBM), pltpu.with_memory_space_constraint(images, pltpu.HBM))


def solution(mesh):
    placed = (P("strip", "along"), P("strip", "along", None))
    return jax.shard_map(
        per_device, mesh=mesh, in_specs=placed, out_specs=P(None, "strip", "along"), check_vma=False
    )
```

```python
import functools
import jax
import jax.numpy as jnp
from jax import lax
from jax.experimental import pallas as pl
from jax.experimental.pallas import tpu as pltpu
from jax.sharding import PartitionSpec as P

F32 = jnp.float32
BF16 = jnp.bfloat16
ROWS, COLS, GROUPS, SUB, LANES = 64, 512, 8, 8, 128
HALF = LANES // 2
RADIUS = 4
UNROLL = 16
COST_ROWS = 16
FIRST_BLOCK = 1
SCALE = -4.0 * 1.4426950408889634


def lane_ids(shape):
    return lax.broadcasted_iota(jnp.int32, shape, len(shape) - 1)


def split3(x):
    hi = x.astype(BF16)
    rest = x - hi.astype(F32)
    mid = rest.astype(BF16)
    low = (rest - mid.astype(F32)).astype(BF16)
    return jnp.concatenate([hi, mid, low], axis=0)


def permuted(x, perm):
    n = x.shape[0]
    out = jnp.dot(split3(x), perm, preferred_element_type=F32)
    return out[:n] + out[n : 2 * n] + out[2 * n :]


def fill_perm(perm_ref, back_ref):
    for k in range(4):
        shape = (128, COLS)
        along = lax.broadcasted_iota(jnp.int32, shape, 1)
        down = lax.broadcasted_iota(jnp.int32, shape, 0) + 128 * k
        rows = pl.ds(128 * k, 128)
        perm_ref[rows, :] = jnp.where(down == 8 * (along & 63) + (along >> 6), 1.0, 0.0).astype(BF16)
        back_ref[rows, :] = jnp.where(along == 8 * (down & 63) + (down >> 6), 1.0, 0.0).astype(BF16)


def spread(x, perm):
    y = permuted(x, perm)
    low = lane_ids((x.shape[0], LANES)) < HALF
    out = []
    for k in range(4):
        v = y[:, LANES * k : LANES * (k + 1)]
        w = pltpu.roll(v, HALF, 1)
        out += [jnp.where(low, v, w), jnp.where(low, w, v)]
    return out


def row_box(x):
    shape = x[0].shape
    pos = lane_ids(shape) & (HALF - 1)
    first, last = pos == 0, pos == HALF - 1
    pre = [x[0]]
    for k in range(1, 8):
        pre.append(pre[-1] + x[k])
    suf = [None] * 8
    suf[7] = x[7]
    for k in range(6, 0, -1):
        suf[k] = suf[k + 1] + x[k]
    suf[0] = pre[7]
    out = []
    for j in range(4):
        out.append(jnp.where(first, 0.0, pltpu.roll(suf[j + 4], 1, 1)) + pre[j + 4])
    for j in range(4, 8):
        out.append(jnp.where(last, 0.0, pltpu.roll(pre[j - 4], LANES - 1, 1)) + suf[j - 4])
    return out


def guide_fields(g, perm, pad_ref, g_ref, a1_ref, a2_ref, i4_ref, mg_ref, inv_ref, then):
    gd = spread(g, perm)
    for j, v in enumerate(widened(gd)):
        g_ref[j] = v
    zero = jnp.zeros((SUB, LANES), F32)
    for j in range(8):
        for n, field in enumerate((gd[j], gd[j] * gd[j])):
            at = 2 * j + n
            pad_ref[at, pl.ds(0, SUB), :] = zero
            pad_ref[at, pl.ds(SUB, ROWS), :] = field
            pad_ref[at, pl.ds(SUB + ROWS, SUB), :] = zero

    then()

    def tile(i, carry):
        base = pl.multiple_of(i * SUB, SUB)
        sums = []
        for at in range(16):
            total = pad_ref[at, pl.ds(base + SUB - RADIUS, SUB), :]
            for k in range(1, 2 * RADIUS + 1):
                total = total + pad_ref[at, pl.ds(base + SUB - RADIUS + k, SUB), :]
            sums.append(total)
        bg, bgg = row_box(sums[0::2]), row_box(sums[1::2])
        shape = (SUB, LANES)
        r = lax.broadcasted_iota(jnp.int32, shape, 0) + base
        nr = jnp.minimum(r + RADIUS, ROWS - 1) - jnp.maximum(r - RADIUS, 0) + 1
        l8 = 8 * (lane_ids(shape) & (HALF - 1))
        for j in range(8):
            c = l8 + j
            nc = jnp.minimum(c + RADIUS, COLS - 1) - jnp.maximum(c - RADIUS, 0) + 1
            inv = 1.0 / (nr * nc).astype(F32)
            mean = bg[j] * inv
            var = bgg[j] * inv - mean * mean
            a1 = (SCALE * inv) / (var + 50.0)
            here = pl.ds(base, SUB)
            a1_ref[j, here, :] = a1
            a2_ref[j, here, :] = a1 * mean
            i4_ref[j, here, :] = SCALE * inv
            mg_ref[j, here, :] = mean
            inv_ref[j, here, :] = inv
        return carry

    lax.fori_loop(0, ROWS // SUB, tile, 0)


def ends(shape):
    pos = lane_ids(shape) & (HALF - 1)
    return pos == 0, pos == HALF - 1


def widened(x):
    first, last = ends(x[0].shape)
    before = [jnp.where(first, 0.0, pltpu.roll(v, 1, 1)) for v in x[4:]]
    after = [jnp.where(last, 0.0, pltpu.roll(v, LANES - 1, 1)) for v in x[:4]]
    return before + list(x) + after


STEP = 24


def forward_table(f, shift, perm, z_ref):
    base = spread(pltpu.roll(f, COLS - shift, 1), perm)
    low = lane_ids((ROWS, LANES)) < HALF
    turned = {(k, 0): base[k] for k in range(8)}
    for k in range(8):
        for q in ((-1,) if k >= 4 else ()) + (1, 2) + ((3,) if k < 3 else ()):
            turned[k, q] = pltpu.roll(base[k], (-q) % LANES, 1)
    for e in range(-4, 19):
        q, k = divmod(e, 8)
        z_ref[pl.ds(e + 4, ROWS, stride=STEP), :] = jnp.where(low, turned[k, q], turned[k, q + 1])


def side_table(s, shift, perm, y_ref):
    base = widened(spread(pltpu.roll(s, ROWS - shift, 0), perm))
    low = lane_ids((SUB, LANES)) < HALF
    for j in range(16):
        tiles = [base[j][SUB * k : SUB * (k + 1)] for k in range(8)]
        for k in range(9):
            y_ref[j, pl.ds(SUB * k, SUB), :] = jnp.where(low, tiles[k % 8], tiles[(k + 1) % 8])


def bcast(ref, j, r):
    return jnp.broadcast_to(ref[j, pl.ds(r, 1), :], (SUB, LANES))


def wide_box(x):
    suf = [x[7]]
    for k in range(6, -1, -1):
        suf.append(suf[-1] + x[k])
    suf.reverse()
    pre = [x[8]]
    for k in range(9, 16):
        pre.append(pre[-1] + x[k])
    return [suf[j] + pre[j] for j in range(8)]


def cost_pass(block, load, masked, g_ref, hx_ref, hy_ref):
    def row(r):
        first, last = ends((SUB, LANES))
        xs, ys = [], []
        for j in range(16):
            g = bcast(g_ref, j, r)
            x = jnp.abs(g - load(r, j))
            if masked and j < 4:
                x = jnp.where(first, 0.0, x)
            if masked and j >= 12:
                x = jnp.where(last, 0.0, x)
            xs.append(x)
            ys.append(g * x)
        for ref, vals in ((hx_ref, xs), (hy_ref, ys)):
            for j, v in enumerate(wide_box(vals)):
                ref[j, r] = v

    def rows_of(k, carry):
        for i in range(COST_ROWS):
            row(k * COST_ROWS + i)
        return carry

    lax.fori_loop(block, ROWS // COST_ROWS, rows_of, 0)


def coef_pass(top, hx_ref, hy_ref, wa_ref, wb_ref, a1_ref, a2_ref, i4_ref, mg_ref):
    low = max(top - RADIUS, 0)
    base = max(low - RADIUS, 0)

    def column(j, carry):
        p, q = hx_ref[j, base], hy_ref[j, base]
        for r in range(base + 1, low + RADIUS):
            p, q = p + hx_ref[j, r], q + hy_ref[j, r]
        old = {}
        wa = wb = None
        for r in range(low, ROWS + RADIUS):
            gone = r - 2 * RADIUS - 1
            if r < ROWS:
                enter, leave = r + RADIUS < ROWS, r - RADIUS - 1 >= base
                if enter and leave:
                    p = p + (hx_ref[j, r + RADIUS] - hx_ref[j, r - RADIUS - 1])
                    q = q + (hy_ref[j, r + RADIUS] - hy_ref[j, r - RADIUS - 1])
                elif enter:
                    p = p + hx_ref[j, r + RADIUS]
                    q = q + hy_ref[j, r + RADIUS]
                else:
                    p = p - hx_ref[j, r - RADIUS - 1]
                    q = q - hy_ref[j, r - RADIUS - 1]
                ca = q * bcast(a1_ref, j, r) - p * bcast(a2_ref, j, r)
                cb = p * bcast(i4_ref, j, r) - ca * bcast(mg_ref, j, r)
                old[r] = ca, cb
                if r == low:
                    wa, wb = ca, cb
                elif gone >= low:
                    wa, wb = wa + (ca - old[gone][0]), wb + (cb - old[gone][1])
                else:
                    wa, wb = wa + ca, wb + cb
            else:
                wa, wb = wa - old[gone][0], wb - old[gone][1]
            if r - RADIUS >= top:
                wa_ref[j, r - RADIUS] = wa
                wb_ref[j, r - RADIUS] = wb
        return carry

    lax.fori_loop(0, 8, column, 0)


def running(x):
    head = [x[0]]
    for k in range(1, 8):
        head.append(head[-1] + x[k])
    tail = [head[7]] + [None] * 6 + [x[7]]
    for k in range(6, 0, -1):
        tail[k] = tail[k + 1] + x[k]
    return head, tail


def score_pass(start, rows, wa_ref, wb_ref, g_ref, inv_ref, sc_ref):
    def row(i, carry):
        r = start + i
        first, last = ends((SUB, LANES))
        ha, ta = running([wa_ref[j, r] for j in range(8)])
        hb, tb = running([wb_ref[j, r] for j in range(8)])
        for j in range(8):
            if j < 4:
                other = ta[j + 4] * bcast(g_ref, j + 12, r) + tb[j + 4]
                other = jnp.where(first, 0.0, pltpu.roll(other, 1, 1))
                same = ha[j + 4] * bcast(g_ref, j + 4, r) + hb[j + 4]
            else:
                other = ha[j - 4] * bcast(g_ref, j - 4, r) + hb[j - 4]
                other = jnp.where(last, 0.0, pltpu.roll(other, LANES - 1, 1))
                same = ta[j - 4] * bcast(g_ref, j + 4, r) + tb[j - 4]
            sc_ref[r, pl.ds(j, SUB, stride=SUB), :] = (same + other) * bcast(inv_ref, j, r)
        return carry

    lax.fori_loop(0, rows, row, 0, unroll=min(UNROLL, rows))


def softmax_pass(start, rows, sc_ref, d_ref, c_ref):
    def row(i, carry):
        r = start + i
        high = lane_ids((SUB, LANES)) >= HALF
        t = [sc_ref[r, pl.ds(SUB * s, SUB), :] for s in range(8)]
        top = t
        while len(top) > 1:
            top = [jnp.maximum(top[k], top[k + 1]) for k in range(0, len(top), 2)]
        top = jnp.maximum(top[0], pltpu.roll(top[0], HALF, 1))
        total = lift = square = None
        for s in range(7, -1, -1):
            w = jnp.exp2(t[s] - top)
            total = w if total is None else total + w
            square = w * w if square is None else square + w * w
            if s:
                lift = total if lift is None else lift + total
        lift = lift + jnp.where(high, 8.0 * total, 0.0)
        total = total + pltpu.roll(total, HALF, 1)
        lift = lift + pltpu.roll(lift, HALF, 1)
        square = square + pltpu.roll(square, HALF, 1)
        unit = 1.0 / total
        d_ref[pl.ds(pl.multiple_of(r * SUB, SUB), SUB), :] = lift * unit
        c_ref[pl.ds(pl.multiple_of(r * SUB, SUB), SUB), :] = square * unit * unit
        return carry

    lax.fori_loop(0, rows, row, 0, unroll=min(UNROLL, rows))


def gathered(start, rows, refs, perm):
    low = lane_ids((rows, LANES)) < HALF
    stacked = []
    for ref in refs:
        parts = []
        for k in range(4):
            even = ref[pl.ds(SUB * start + 2 * k, rows, stride=SUB), :]
            odd = ref[pl.ds(SUB * start + 2 * k + 1, rows, stride=SUB), :]
            parts.append(jnp.where(low, even, odd))
        stacked.append(jnp.concatenate(parts, axis=1))
    return permuted(jnp.concatenate(stacked, axis=0), perm)


SCRATCH = dict(
    perm=((COLS, COLS), BF16), back=((COLS, COLS), BF16), pad=((16, ROWS + 16, LANES), F32),
    g=((16, ROWS, LANES), F32), a1=((8, ROWS, LANES), F32), a2=((8, ROWS, LANES), F32),
    i4=((8, ROWS, LANES), F32), mg=((16, ROWS, LANES), F32), inv=((8, ROWS, LANES), F32),
    z=((24 * ROWS, LANES), F32), y=((16, ROWS + SUB, LANES), F32),
    hx=((8, ROWS, SUB, LANES), F32), hy=((8, ROWS, SUB, LANES), F32),
    wa=((8, ROWS, SUB, LANES), F32), wb=((8, ROWS, SUB, LANES), F32),
    sc=((ROWS, SUB * SUB, LANES), F32), d=((ROWS * SUB, LANES), F32), c=((ROWS * SUB, LANES), F32),
)


def load_forward(b):
    return lambda r, j: b["z"][pl.ds(r * STEP + j, SUB), :]


def load_side(b):
    return lambda r, j: b["y"][j, pl.ds(r, SUB), :]


MESH = pl.DeviceIdType.MESH
PIECES = 4
SENT = 2


def kernel(offsets_ref, images_ref, out_ref, *refs):
    names = list(SCRATCH)
    b = dict(zip(names, refs))
    own, f_in, s_in, b_in, b_shift, shifts, back_shifts, here, sent, got = refs[len(names) :]
    perm = b["perm"]
    axes = {name: (lax.axis_index(name), lax.axis_size(name)) for name in ("along", "strip")}

    barrier = pltpu.get_barrier_semaphore()
    for axis, (at, count) in axes.items():

        @pl.when(at < count - 1)
        def _():
            pl.semaphore_signal(barrier, inc=1, device_id={axis: at + 1}, device_id_type=MESH)

    load_own = pltpu.make_async_copy(images_ref, own, here.at[0])
    load_own.start()
    load_shifts = pltpu.make_async_copy(offsets_ref, shifts, here.at[1])
    load_shifts.start()
    fill_perm(perm, b["back"])
    plan = (("along", f_in, 0), ("strip", s_in, 4))
    for axis, landing, base in plan:
        at, count = axes[axis]

        @pl.when(at == count - 1)
        def _():
            landing[...] = jnp.zeros_like(landing)

        @pl.when(at == 0)
        def _():
            out_ref[pl.ds(base + 2, 2)] = jnp.zeros((2, ROWS, COLS), F32)

    ready = sum((at > 0).astype(jnp.int32) for at, _ in axes.values())

    @pl.when(ready > 0)
    def _():
        pl.semaphore_wait(barrier, ready)


    def send(axis, step, src, dst, slot):
        at, _ = axes[axis]
        return pltpu.make_async_remote_copy(
            src_ref=src, dst_ref=dst, send_sem=sent.at[slot], recv_sem=got.at[slot],
            device_id={axis: at + step}, device_id_type=MESH)

    image_copies = [send(axis, -1, images_ref, landing, slot) for slot, (axis, landing, _) in enumerate(plan)]

    def start_image(which, also=True):
        at, _ = axes[plan[which][0]]
        pl.when(jnp.logical_and(at > 0, also))(image_copies[which].start)

    def await_image(which):
        at, count = axes[plan[which][0]]
        pl.when(at < count - 1)(image_copies[which].wait_recv)

    odd = lax.rem(axes["along"][0], 2)
    start_image(0, odd == 1)
    start_image(1, odd == 1)
    load_own.wait()
    load_shifts.wait()
    guide_fields(own[...], perm[...], b["pad"], b["g"], b["a1"], b["a2"], b["i4"], b["mg"], b["inv"], lambda: start_image(0, odd == 0))
    rows = ROWS // PIECES
    along, alongs = axes["along"]
    gives_back = jnp.logical_and(odd == 1, along < alongs - 1)
    gets_back = jnp.logical_and(odd == 0, along > 0)
    back_copies = [
        send("along", 1, images_ref, b_in, 2 + 2 * PIECES),
        send("along", 1, offsets_ref, b_shift, 3 + 2 * PIECES),
    ]

    def piece_copy(which, piece):
        axis, _, base = plan[which]
        span = pl.ds(pl.multiple_of(piece * rows, rows), rows)
        return send(
            axis, 1, out_ref.at[pl.ds(base, 2), span, :], out_ref.at[pl.ds(base + 2, 2), span, :],
            2 + which * PIECES + piece)

    def pair(step):
        which = jnp.where(step == 2, 2, lax.rem(step + odd, 2))

        @pl.when(jnp.logical_and(step == 0, odd == 0))
        def _():
            await_image(0)

        @pl.when(which == 2)
        def _():
            for copy in back_copies:
                copy.wait_recv()
            local = pltpu.make_async_copy(b_shift, back_shifts, here.at[2])
            local.start()
            f_in[...] = own[...]
            local.wait()
            guide_fields(b_in[...], perm[...], b["pad"], b["g"], b["a1"], b["a2"], b["i4"], b["mg"], b["inv"], lambda: None)

        @pl.when(which != 1)
        def _():
            shift = jnp.where(which == 2, back_shifts[0, 0, 0], shifts[0, 0, 0])
            forward_table(f_in[...], shift, perm[...], b["z"])
            start_image(1, jnp.logical_and(step == 0, odd == 0))
            cost_pass(which // 2 * FIRST_BLOCK, load_forward(b), True, b["g"], b["hx"], b["hy"])

        @pl.when(which == 1)
        def _():
            await_image(1)
            side_table(s_in[...], shifts[0, 0, 1], perm[...], b["y"])
            cost_pass(0, load_side(b), False, b["g"], b["hx"], b["hy"])

        @pl.when(which < 2)
        def _():
            coef_pass(0, b["hx"], b["hy"], b["wa"], b["wb"], b["a1"], b["a2"], b["i4"], b["mg"])

        @pl.when(which == 2)
        def _():
            coef_pass(SENT * rows, b["hx"], b["hy"], b["wa"], b["wb"], b["a1"], b["a2"], b["i4"], b["mg"])

        @pl.when(jnp.logical_and(step == 0, odd == 1))
        def _():
            await_image(0)

            @pl.when(gives_back)
            def _():
                for copy in back_copies:
                    copy.start()

        base = 4 * which - 6 * (which // 2)

        def piece_of(piece, inner):
            start = pl.multiple_of(piece * rows, rows)
            score_pass(start, rows, b["wa"], b["wb"], b["g"], b["inv"], b["sc"])
            softmax_pass(start, rows, b["sc"], b["d"], b["c"])
            both = gathered(start, rows, (b["d"], b["c"]), b["back"][...])
            span = pl.ds(start, rows)
            out_ref[base, span, :] = both[:rows]
            out_ref[base + 1, span, :] = both[rows:]
            wanted = jnp.logical_or(odd == 0, jnp.logical_and(gives_back, piece < SENT))
            pl.when(jnp.logical_and(which == 0, wanted))(piece_copy(0, piece).start)
            at, count = axes["strip"]
            pl.when(jnp.logical_and(which == 1, at < count - 1))(piece_copy(1, piece).start)
            return inner

        lax.fori_loop(which // 2 * SENT, PIECES, piece_of, 0)

    def turn(step, carry):
        pl.when(jnp.logical_or(step < 2, gets_back))(lambda: pair(step))
        return carry

    lax.fori_loop(0, 3, turn, 0)

    for which, (axis, _, _) in enumerate(plan):
        at, count = axes[axis]
        pl.when(at > 0)(image_copies[which].wait_send)
        for piece in range(PIECES):
            near = which == 0 and piece >= SENT
            gives, gets = (odd == 0, odd == 1) if near else (at < count - 1, at > 0)
            copy = piece_copy(which, piece)
            pl.when(gives)(copy.wait_send)
            pl.when(gets)(copy.wait_recv)
    for copy in back_copies:
        pl.when(gives_back)(copy.wait_send)


def per_device(images, offsets):
    slots = 4 + 2 * PIECES
    return pl.pallas_call(
        kernel,
        out_shape=jax.ShapeDtypeStruct((8, ROWS, COLS), F32),
        in_specs=[pl.BlockSpec(memory_space=pltpu.HBM), pl.BlockSpec(memory_space=pltpu.HBM)],
        out_specs=pl.BlockSpec(memory_space=pltpu.VMEM),
        scratch_shapes=[pltpu.VMEM(*v) for v in SCRATCH.values()]
        + [pltpu.VMEM((ROWS, COLS), F32)] * 4
        + [
            pltpu.VMEM((1, 1, 2), jnp.int32),
            pltpu.SMEM((1, 1, 2), jnp.int32),
            pltpu.SMEM((1, 1, 2), jnp.int32),
            pltpu.SemaphoreType.DMA((3,)),
            pltpu.SemaphoreType.DMA((slots,)),
            pltpu.SemaphoreType.DMA((slots,)),
        ],
        compiler_params=pltpu.CompilerParams(collective_id=0, has_side_effects=True, vmem_limit_bytes=48 << 20),
    )(pltpu.with_memory_space_constraint(offsets, pltpu.HBM), pltpu.with_memory_space_constraint(images, pltpu.HBM))


def solution(mesh):
    placed = (P("strip", "along"), P("strip", "along", None))
    return jax.shard_map(
        per_device, mesh=mesh, in_specs=placed, out_specs=P(None, "strip", "along"), check_vma=False
    )
```

```python
import functools
import jax
import jax.numpy as jnp
from jax import lax
from jax.experimental import pallas as pl
from jax.experimental.pallas import tpu as pltpu
from jax.sharding import PartitionSpec as P

F32 = jnp.float32
BF16 = jnp.bfloat16
ROWS, COLS, GROUPS, SUB, LANES = 64, 512, 8, 8, 128
HALF = LANES // 2
RADIUS = 4
UNROLL = 16
COST_ROWS = 16
FIRST_BLOCK = 1
SCALE = -4.0 * 1.4426950408889634


def lane_ids(shape):
    return lax.broadcasted_iota(jnp.int32, shape, len(shape) - 1)


def split3(x):
    hi = x.astype(BF16)
    rest = x - hi.astype(F32)
    mid = rest.astype(BF16)
    low = (rest - mid.astype(F32)).astype(BF16)
    return jnp.concatenate([hi, mid, low], axis=0)


def permuted(x, perm):
    n = x.shape[0]
    out = jnp.dot(split3(x), perm, preferred_element_type=F32)
    return out[:n] + out[n : 2 * n] + out[2 * n :]


def fill_perm(perm_ref, back_ref):
    for k in range(4):
        shape = (128, COLS)
        along = lax.broadcasted_iota(jnp.int32, shape, 1)
        down = lax.broadcasted_iota(jnp.int32, shape, 0) + 128 * k
        rows = pl.ds(128 * k, 128)
        perm_ref[rows, :] = jnp.where(down == 8 * (along & 63) + (along >> 6), 1.0, 0.0).astype(BF16)
        back_ref[rows, :] = jnp.where(along == 8 * (down & 63) + (down >> 6), 1.0, 0.0).astype(BF16)


def spread(x, perm):
    y = permuted(x, perm)
    low = lane_ids((x.shape[0], LANES)) < HALF
    out = []
    for k in range(4):
        v = y[:, LANES * k : LANES * (k + 1)]
        w = pltpu.roll(v, HALF, 1)
        out += [jnp.where(low, v, w), jnp.where(low, w, v)]
    return out


def row_box(x):
    shape = x[0].shape
    pos = lane_ids(shape) & (HALF - 1)
    first, last = pos == 0, pos == HALF - 1
    pre = [x[0]]
    for k in range(1, 8):
        pre.append(pre[-1] + x[k])
    suf = [None] * 8
    suf[7] = x[7]
    for k in range(6, 0, -1):
        suf[k] = suf[k + 1] + x[k]
    suf[0] = pre[7]
    out = []
    for j in range(4):
        out.append(jnp.where(first, 0.0, pltpu.roll(suf[j + 4], 1, 1)) + pre[j + 4])
    for j in range(4, 8):
        out.append(jnp.where(last, 0.0, pltpu.roll(pre[j - 4], LANES - 1, 1)) + suf[j - 4])
    return out


def guide_fields(g, perm, pad_ref, g_ref, a1_ref, a2_ref, i4_ref, mg_ref, inv_ref, then, tile_from=0):
    gd = spread(g, perm)
    for j, v in enumerate(widened(gd)):
        g_ref[j] = v
    zero = jnp.zeros((SUB, LANES), F32)
    for j in range(8):
        for n, field in enumerate((gd[j], gd[j] * gd[j])):
            at = 2 * j + n
            pad_ref[at, pl.ds(0, SUB), :] = zero
            pad_ref[at, pl.ds(SUB, ROWS), :] = field
            pad_ref[at, pl.ds(SUB + ROWS, SUB), :] = zero

    then()

    def tile(i, carry):
        base = pl.multiple_of(i * SUB, SUB)
        sums = []
        for at in range(16):
            total = pad_ref[at, pl.ds(base + SUB - RADIUS, SUB), :]
            for k in range(1, 2 * RADIUS + 1):
                total = total + pad_ref[at, pl.ds(base + SUB - RADIUS + k, SUB), :]
            sums.append(total)
        bg, bgg = row_box(sums[0::2]), row_box(sums[1::2])
        shape = (SUB, LANES)
        r = lax.broadcasted_iota(jnp.int32, shape, 0) + base
        nr = jnp.minimum(r + RADIUS, ROWS - 1) - jnp.maximum(r - RADIUS, 0) + 1
        l8 = 8 * (lane_ids(shape) & (HALF - 1))
        for j in range(8):
            c = l8 + j
            nc = jnp.minimum(c + RADIUS, COLS - 1) - jnp.maximum(c - RADIUS, 0) + 1
            inv = 1.0 / (nr * nc).astype(F32)
            mean = bg[j] * inv
            var = bgg[j] * inv - mean * mean
            a1 = (SCALE * inv) / (var + 50.0)
            here = pl.ds(base, SUB)
            a1_ref[j, here, :] = a1
            a2_ref[j, here, :] = a1 * mean
            i4_ref[j, here, :] = SCALE * inv
            mg_ref[j, here, :] = mean
            inv_ref[j, here, :] = inv
        return carry

    lax.fori_loop(tile_from, ROWS // SUB, tile, 0)


def ends(shape):
    pos = lane_ids(shape) & (HALF - 1)
    return pos == 0, pos == HALF - 1


def widened(x):
    first, last = ends(x[0].shape)
    before = [jnp.where(first, 0.0, pltpu.roll(v, 1, 1)) for v in x[4:]]
    after = [jnp.where(last, 0.0, pltpu.roll(v, LANES - 1, 1)) for v in x[:4]]
    return before + list(x) + after


STEP = 24


def forward_table(f, shift, perm, z_ref):
    base = spread(pltpu.roll(f, COLS - shift, 1), perm)
    low = lane_ids((ROWS, LANES)) < HALF
    turned = {(k, 0): base[k] for k in range(8)}
    for k in range(8):
        for q in ((-1,) if k >= 4 else ()) + (1, 2) + ((3,) if k < 3 else ()):
            turned[k, q] = pltpu.roll(base[k], (-q) % LANES, 1)
    for e in range(-4, 19):
        q, k = divmod(e, 8)
        z_ref[pl.ds(e + 4, ROWS, stride=STEP), :] = jnp.where(low, turned[k, q], turned[k, q + 1])


def side_table(s, shift, perm, y_ref):
    base = widened(spread(pltpu.roll(s, ROWS - shift, 0), perm))
    low = lane_ids((SUB, LANES)) < HALF
    for j in range(16):
        tiles = [base[j][SUB * k : SUB * (k + 1)] for k in range(8)]
        for k in range(9):
            y_ref[j, pl.ds(SUB * k, SUB), :] = jnp.where(low, tiles[k % 8], tiles[(k + 1) % 8])


def bcast(ref, j, r):
    return jnp.broadcast_to(ref[j, pl.ds(r, 1), :], (SUB, LANES))


def wide_box(x):
    suf = [x[7]]
    for k in range(6, -1, -1):
        suf.append(suf[-1] + x[k])
    suf.reverse()
    pre = [x[8]]
    for k in range(9, 16):
        pre.append(pre[-1] + x[k])
    return [suf[j] + pre[j] for j in range(8)]


def cost_pass(block, load, masked, g_ref, hx_ref, hy_ref):
    def row(r):
        first, last = ends((SUB, LANES))
        xs, ys = [], []
        for j in range(16):
            g = bcast(g_ref, j, r)
            x = jnp.abs(g - load(r, j))
            if masked and j < 4:
                x = jnp.where(first, 0.0, x)
            if masked and j >= 12:
                x = jnp.where(last, 0.0, x)
            xs.append(x)
            ys.append(g * x)
        for ref, vals in ((hx_ref, xs), (hy_ref, ys)):
            for j, v in enumerate(wide_box(vals)):
                ref[j, r] = v

    def rows_of(k, carry):
        for i in range(COST_ROWS):
            row(k * COST_ROWS + i)
        return carry

    lax.fori_loop(block, ROWS // COST_ROWS, rows_of, 0)


def coef_pass(top, hx_ref, hy_ref, wa_ref, wb_ref, a1_ref, a2_ref, i4_ref, mg_ref):
    low = max(top - RADIUS, 0)
    base = max(low - RADIUS, 0)

    def column(j, carry):
        p, q = hx_ref[j, base], hy_ref[j, base]
        for r in range(base + 1, low + RADIUS):
            p, q = p + hx_ref[j, r], q + hy_ref[j, r]
        old = {}
        wa = wb = None
        for r in range(low, ROWS + RADIUS):
            gone = r - 2 * RADIUS - 1
            if r < ROWS:
                enter, leave = r + RADIUS < ROWS, r - RADIUS - 1 >= base
                if enter and leave:
                    p = p + (hx_ref[j, r + RADIUS] - hx_ref[j, r - RADIUS - 1])
                    q = q + (hy_ref[j, r + RADIUS] - hy_ref[j, r - RADIUS - 1])
                elif enter:
                    p = p + hx_ref[j, r + RADIUS]
                    q = q + hy_ref[j, r + RADIUS]
                else:
                    p = p - hx_ref[j, r - RADIUS - 1]
                    q = q - hy_ref[j, r - RADIUS - 1]
                ca = q * bcast(a1_ref, j, r) - p * bcast(a2_ref, j, r)
                cb = p * bcast(i4_ref, j, r) - ca * bcast(mg_ref, j, r)
                old[r] = ca, cb
                if r == low:
                    wa, wb = ca, cb
                elif gone >= low:
                    wa, wb = wa + (ca - old[gone][0]), wb + (cb - old[gone][1])
                else:
                    wa, wb = wa + ca, wb + cb
            else:
                wa, wb = wa - old[gone][0], wb - old[gone][1]
            if r - RADIUS >= top:
                wa_ref[j, r - RADIUS] = wa
                wb_ref[j, r - RADIUS] = wb
        return carry

    lax.fori_loop(0, 8, column, 0)


def running(x):
    head = [x[0]]
    for k in range(1, 8):
        head.append(head[-1] + x[k])
    tail = [head[7]] + [None] * 6 + [x[7]]
    for k in range(6, 0, -1):
        tail[k] = tail[k + 1] + x[k]
    return head, tail


def score_pass(start, rows, wa_ref, wb_ref, g_ref, inv_ref, sc_ref):
    def row(i, carry):
        r = start + i
        first, last = ends((SUB, LANES))
        ha, ta = running([wa_ref[j, r] for j in range(8)])
        hb, tb = running([wb_ref[j, r] for j in range(8)])
        for j in range(8):
            if j < 4:
                other = ta[j + 4] * bcast(g_ref, j + 12, r) + tb[j + 4]
                other = jnp.where(first, 0.0, pltpu.roll(other, 1, 1))
                same = ha[j + 4] * bcast(g_ref, j + 4, r) + hb[j + 4]
            else:
                other = ha[j - 4] * bcast(g_ref, j - 4, r) + hb[j - 4]
                other = jnp.where(last, 0.0, pltpu.roll(other, LANES - 1, 1))
                same = ta[j - 4] * bcast(g_ref, j + 4, r) + tb[j - 4]
            sc_ref[r, pl.ds(j, SUB, stride=SUB), :] = (same + other) * bcast(inv_ref, j, r)
        return carry

    lax.fori_loop(0, rows, row, 0, unroll=min(UNROLL, rows))


def softmax_pass(start, rows, sc_ref, d_ref, c_ref):
    def row(i, carry):
        r = start + i
        high = lane_ids((SUB, LANES)) >= HALF
        t = [sc_ref[r, pl.ds(SUB * s, SUB), :] for s in range(8)]
        top = t
        while len(top) > 1:
            top = [jnp.maximum(top[k], top[k + 1]) for k in range(0, len(top), 2)]
        top = jnp.maximum(top[0], pltpu.roll(top[0], HALF, 1))
        total = lift = square = None
        for s in range(7, -1, -1):
            w = jnp.exp2(t[s] - top)
            total = w if total is None else total + w
            square = w * w if square is None else square + w * w
            if s:
                lift = total if lift is None else lift + total
        lift = lift + jnp.where(high, 8.0 * total, 0.0)
        total = total + pltpu.roll(total, HALF, 1)
        lift = lift + pltpu.roll(lift, HALF, 1)
        square = square + pltpu.roll(square, HALF, 1)
        unit = 1.0 / total
        d_ref[pl.ds(pl.multiple_of(r * SUB, SUB), SUB), :] = lift * unit
        c_ref[pl.ds(pl.multiple_of(r * SUB, SUB), SUB), :] = square * unit * unit
        return carry

    lax.fori_loop(0, rows, row, 0, unroll=min(UNROLL, rows))


def gathered(start, rows, refs, perm):
    low = lane_ids((rows, LANES)) < HALF
    stacked = []
    for ref in refs:
        parts = []
        for k in range(4):
            even = ref[pl.ds(SUB * start + 2 * k, rows, stride=SUB), :]
            odd = ref[pl.ds(SUB * start + 2 * k + 1, rows, stride=SUB), :]
            parts.append(jnp.where(low, even, odd))
        stacked.append(jnp.concatenate(parts, axis=1))
    return permuted(jnp.concatenate(stacked, axis=0), perm)


SCRATCH = dict(
    perm=((COLS, COLS), BF16), back=((COLS, COLS), BF16), pad=((16, ROWS + 16, LANES), F32),
    g=((16, ROWS, LANES), F32), a1=((8, ROWS, LANES), F32), a2=((8, ROWS, LANES), F32),
    i4=((8, ROWS, LANES), F32), mg=((16, ROWS, LANES), F32), inv=((8, ROWS, LANES), F32),
    z=((24 * ROWS, LANES), F32), y=((16, ROWS + SUB, LANES), F32),
    hx=((8, ROWS, SUB, LANES), F32), hy=((8, ROWS, SUB, LANES), F32),
    wa=((8, ROWS, SUB, LANES), F32), wb=((8, ROWS, SUB, LANES), F32),
    sc=((ROWS, SUB * SUB, LANES), F32), d=((ROWS * SUB, LANES), F32), c=((ROWS * SUB, LANES), F32),
)


def load_forward(b):
    return lambda r, j: b["z"][pl.ds(r * STEP + j, SUB), :]


def load_side(b):
    return lambda r, j: b["y"][j, pl.ds(r, SUB), :]


MESH = pl.DeviceIdType.MESH
PIECES = 4
SENT = 2


def kernel(offsets_ref, images_ref, out_ref, *refs):
    names = list(SCRATCH)
    b = dict(zip(names, refs))
    own, f_in, s_in, b_in, b_shift, shifts, back_shifts, here, sent, got = refs[len(names) :]
    perm = b["perm"]
    axes = {name: (lax.axis_index(name), lax.axis_size(name)) for name in ("along", "strip")}

    barrier = pltpu.get_barrier_semaphore()
    for axis, (at, count) in axes.items():

        @pl.when(at < count - 1)
        def _():
            pl.semaphore_signal(barrier, inc=1, device_id={axis: at + 1}, device_id_type=MESH)

    load_own = pltpu.make_async_copy(images_ref, own, here.at[0])
    load_own.start()
    load_shifts = pltpu.make_async_copy(offsets_ref, shifts, here.at[1])
    load_shifts.start()
    fill_perm(perm, b["back"])
    plan = (("along", f_in, 0), ("strip", s_in, 4))
    for axis, landing, base in plan:
        at, count = axes[axis]

        @pl.when(at == count - 1)
        def _():
            landing[...] = jnp.zeros_like(landing)

        @pl.when(at == 0)
        def _():
            out_ref[pl.ds(base + 2, 2)] = jnp.zeros((2, ROWS, COLS), F32)

    ready = sum((at > 0).astype(jnp.int32) for at, _ in axes.values())

    @pl.when(ready > 0)
    def _():
        pl.semaphore_wait(barrier, ready)


    def send(axis, step, src, dst, slot):
        at, _ = axes[axis]
        return pltpu.make_async_remote_copy(
            src_ref=src, dst_ref=dst, send_sem=sent.at[slot], recv_sem=got.at[slot],
            device_id={axis: at + step}, device_id_type=MESH)

    image_copies = [send(axis, -1, images_ref, landing, slot) for slot, (axis, landing, _) in enumerate(plan)]

    def start_image(which, also=True):
        at, _ = axes[plan[which][0]]
        pl.when(jnp.logical_and(at > 0, also))(image_copies[which].start)

    def await_image(which):
        at, count = axes[plan[which][0]]
        pl.when(at < count - 1)(image_copies[which].wait_recv)

    odd = lax.rem(axes["along"][0], 2)
    start_image(0)
    start_image(1, odd == 1)
    load_own.wait()
    load_shifts.wait()
    guide_fields(own[...], perm[...], b["pad"], b["g"], b["a1"], b["a2"], b["i4"], b["mg"], b["inv"], lambda: None)
    rows = ROWS // PIECES
    along, alongs = axes["along"]
    gives_back = jnp.logical_and(odd == 1, along < alongs - 1)
    gets_back = jnp.logical_and(odd == 0, along > 0)
    back_copies = [
        send("along", 1, images_ref, b_in, 2 + 2 * PIECES),
        send("along", 1, offsets_ref, b_shift, 3 + 2 * PIECES),
    ]

    def piece_copy(which, piece):
        axis, _, base = plan[which]
        span = pl.ds(pl.multiple_of(piece * rows, rows), rows)
        return send(
            axis, 1, out_ref.at[pl.ds(base, 2), span, :], out_ref.at[pl.ds(base + 2, 2), span, :],
            2 + which * PIECES + piece)

    def pair(step):
        which = jnp.where(step == 2, 2, lax.rem(step + odd, 2))

        @pl.when(jnp.logical_and(step == 0, odd == 0))
        def _():
            await_image(0)

        @pl.when(which == 2)
        def _():
            for copy in back_copies:
                copy.wait_recv()
            local = pltpu.make_async_copy(b_shift, back_shifts, here.at[2])
            local.start()
            f_in[...] = own[...]
            local.wait()
            guide_fields(b_in[...], perm[...], b["pad"], b["g"], b["a1"], b["a2"], b["i4"], b["mg"], b["inv"], lambda: None, max(SENT * rows // SUB - 1, 0))

        @pl.when(which != 1)
        def _():
            shift = jnp.where(which == 2, back_shifts[0, 0, 0], shifts[0, 0, 0])
            forward_table(f_in[...], shift, perm[...], b["z"])
            start_image(1, jnp.logical_and(step == 0, odd == 0))
            cost_pass(which // 2 * FIRST_BLOCK, load_forward(b), True, b["g"], b["hx"], b["hy"])

        @pl.when(which == 1)
        def _():
            await_image(1)
            side_table(s_in[...], shifts[0, 0, 1], perm[...], b["y"])
            cost_pass(0, load_side(b), False, b["g"], b["hx"], b["hy"])

        @pl.when(which < 2)
        def _():
            coef_pass(0, b["hx"], b["hy"], b["wa"], b["wb"], b["a1"], b["a2"], b["i4"], b["mg"])

        @pl.when(which == 2)
        def _():
            coef_pass(SENT * rows, b["hx"], b["hy"], b["wa"], b["wb"], b["a1"], b["a2"], b["i4"], b["mg"])

        @pl.when(jnp.logical_and(step == 0, odd == 1))
        def _():
            await_image(0)

            @pl.when(gives_back)
            def _():
                for copy in back_copies:
                    copy.start()

        base = 4 * which - 6 * (which // 2)

        def piece_of(piece, inner):
            start = pl.multiple_of(piece * rows, rows)
            score_pass(start, rows, b["wa"], b["wb"], b["g"], b["inv"], b["sc"])
            softmax_pass(start, rows, b["sc"], b["d"], b["c"])
            both = gathered(start, rows, (b["d"], b["c"]), b["back"][...])
            span = pl.ds(start, rows)
            out_ref[base, span, :] = both[:rows]
            out_ref[base + 1, span, :] = both[rows:]
            wanted = jnp.logical_or(odd == 0, jnp.logical_and(gives_back, piece < SENT))
            pl.when(jnp.logical_and(which == 0, wanted))(piece_copy(0, piece).start)
            at, count = axes["strip"]
            pl.when(jnp.logical_and(which == 1, at < count - 1))(piece_copy(1, piece).start)
            return inner

        lax.fori_loop(which // 2 * SENT, PIECES, piece_of, 0)

    def turn(step, carry):
        pl.when(jnp.logical_or(step < 2, gets_back))(lambda: pair(step))
        return carry

    lax.fori_loop(0, 3, turn, 0)

    for which, (axis, _, _) in enumerate(plan):
        at, count = axes[axis]
        pl.when(at > 0)(image_copies[which].wait_send)
        for piece in range(PIECES):
            near = which == 0 and piece >= SENT
            gives, gets = (odd == 0, odd == 1) if near else (at < count - 1, at > 0)
            copy = piece_copy(which, piece)
            pl.when(gives)(copy.wait_send)
            pl.when(gets)(copy.wait_recv)
    for copy in back_copies:
        pl.when(gives_back)(copy.wait_send)


def per_device(images, offsets):
    slots = 4 + 2 * PIECES
    return pl.pallas_call(
        kernel,
        out_shape=jax.ShapeDtypeStruct((8, ROWS, COLS), F32),
        in_specs=[pl.BlockSpec(memory_space=pltpu.HBM), pl.BlockSpec(memory_space=pltpu.HBM)],
        out_specs=pl.BlockSpec(memory_space=pltpu.VMEM),
        scratch_shapes=[pltpu.VMEM(*v) for v in SCRATCH.values()]
        + [pltpu.VMEM((ROWS, COLS), F32)] * 4
        + [
            pltpu.VMEM((1, 1, 2), jnp.int32),
            pltpu.SMEM((1, 1, 2), jnp.int32),
            pltpu.SMEM((1, 1, 2), jnp.int32),
            pltpu.SemaphoreType.DMA((3,)),
            pltpu.SemaphoreType.DMA((slots,)),
            pltpu.SemaphoreType.DMA((slots,)),
        ],
        compiler_params=pltpu.CompilerParams(collective_id=0, has_side_effects=True, vmem_limit_bytes=48 << 20),
    )(pltpu.with_memory_space_constraint(offsets, pltpu.HBM), pltpu.with_memory_space_constraint(images, pltpu.HBM))


def solution(mesh):
    placed = (P("strip", "along"), P("strip", "along", None))
    return jax.shard_map(
        per_device, mesh=mesh, in_specs=placed, out_specs=P(None, "strip", "along"), check_vma=False
    )
```
